256 devices in a mesh: ctx: 64 (over y, z_hi, x, core), ch: 4 (over z_lo).
Axes of the slice: x: 4, y: 4, z: 8 (z_hi: 2, z_lo: 4; z = z_hi * 4 + z_lo), core: 2. Of those that a mesh axis runs over, the one named last changes fastest.
Arguments:
- query_short: bfloat16 [8192, 8192], P('ctx', 'ch'), may hold values from -6 to 6
- key_short: bfloat16 [8192, 8192], P('ctx', 'ch'), may hold values from -6 to 6
- value_short: bfloat16 [8192, 8192], P('ctx', 'ch'), may hold values from -6 to 6
- short_taps: float32 [128, 8192], P(None, 'ch'), may hold values from -0.5 to 0.5
- query_long: bfloat16 [8192, 8192], P('ctx', 'ch'), may hold values from -6 to 6
- key_long: bfloat16 [8192, 8192], P('ctx', 'ch'), may hold values from -6 to 6
- long_residue: float32 [16, 8192], P(None, 'ch'), may hold values from -0.15625 to 0.15625
- long_rate: float32 [16, 8192], P(None, 'ch'), may hold values from 0.00012207031 to 0.05
- cotangent: bfloat16 [8192, 8192], P('ctx', 'ch'), may hold values from -6 to 6
Outputs:
- core_output: bfloat16 [8192, 8192], P('ctx', 'ch')
- query_short_grad: bfloat16 [8192, 8192], P('ctx', 'ch')
- key_short_grad: bfloat16 [8192, 8192], P('ctx', 'ch')
- value_short_grad: bfloat16 [8192, 8192], P('ctx', 'ch')
- query_long_grad: bfloat16 [8192, 8192], P('ctx', 'ch')
- key_long_grad: bfloat16 [8192, 8192], P('ctx', 'ch')
- taps_grad: float32 [128, 8192], P(None, 'ch')
The draws below stay inside these ranges and needn't reach their ends.
All inputs are finite; a program needn't handle non-finite values.
Results may differ from the reference program's by a relative error of at most 0.0064.
Values may be sent and summed in bfloat16 or wider, within the bound.
A program may use at most 128 MiB of HBM per device.

```python
import math
import jax
import jax.numpy as jnp
from jax import lax

D = 8192
MR_LEN = 128
MODES = 16
SEQ = 8192


def steps_of(key, extent, shards, least, largest):
    loudness = 1.0
    for position, shards_of in shards:
        heights = jax.random.uniform(jax.random.fold_in(jax.random.fold_in(key, 6), position), (shards_of,), jnp.float32, least / len(shards), largest / len(shards))
        loudness = loudness * jnp.repeat(jnp.exp(heights), extent[position] // shards_of).reshape((-1,) + (1,) * (len(extent) - 1 - position))
    return loudness


def gaussian(stream_key, dims, deviation, bound, shards=(), held_as=jnp.bfloat16):
    values = jax.random.normal(stream_key, dims, jnp.float32) * deviation
    if len(shards) > 0:
        values = steps_of(stream_key, dims, shards, -0.22, 0.18) * values
    return jnp.clip(values, min=-bound, max=bound).astype(held_as)


def setup_inputs(seed: int = 0) -> dict:
    key_list = jax.random.split(jax.random.key(seed), 10)
    query_short = gaussian(key_list[0], (SEQ, D), 1.0, 6.0, ((0, 64), (1, 4)))
    key_short = gaussian(key_list[1], (SEQ, D), 1.0, 6.0, ((0, 64), (1, 4)))
    value_short = gaussian(key_list[2], (SEQ, D), 1.0, 6.0, ((0, 64), (1, 4)))
    short_taps = gaussian(key_list[3], (MR_LEN, D), MR_LEN ** -0.5, 0.5, ((1, 4),), jnp.float32)
    query_long = gaussian(key_list[4], (SEQ, D), 1.0, 6.0, ((0, 64), (1, 4)))
    key_long = gaussian(key_list[5], (SEQ, D), 1.0, 6.0, ((0, 64), (1, 4)))
    long_residue = gaussian(key_list[6], (MODES, D), (1.0 / SEQ ** 0.5), 0.15625, ((1, 4),), jnp.float32)
    long_rate = jnp.clip(jnp.exp(math.log(0.05) - 6.015181 * jax.random.uniform(key_list[7], (MODES, D), jnp.float32) ** steps_of(key_list[7], (MODES, D), ((1, 4),), -0.2, 0.2)), 0.00012207031, 0.05)
    cotangent = gaussian(key_list[8], (SEQ, D), 1.0, 6.0, ((0, 64), (1, 4)))
    return dict(query_short=query_short, key_short=key_short, value_short=value_short, short_taps=short_taps, query_long=query_long, key_long=key_long, long_residue=long_residue, long_rate=long_rate, cotangent=cotangent)


def settled(value):
    return lax.optimization_barrier(value.astype(jnp.bfloat16)).astype(jnp.float32)


def causal_apply(signal, kernel, total, keep):
    spectrum = jnp.fft.rfft(signal, total, axis=0) * jnp.fft.rfft(kernel, total, axis=0)
    return jnp.fft.irfft(spectrum, total, axis=0)[:keep]


def correlate(signal, kernel, total, keep):
    spectrum = jnp.fft.rfft(signal, total, axis=0) * jnp.conj(jnp.fft.rfft(kernel, total, axis=0))
    return jnp.fft.irfft(spectrum, total, axis=0)[:keep]


def channel_block(inputs):
    short_q, short_k, short_v, taps_block, long_q, long_k, residue_block, rate_block, upstream = inputs
    short_q = short_q.astype(jnp.float32)
    short_k = short_k.astype(jnp.float32)
    short_v = short_v.astype(jnp.float32)
    long_q = long_q.astype(jnp.float32)
    long_k = long_k.astype(jnp.float32)
    upstream = upstream.astype(jnp.float32)
    total = 2 * SEQ
    short_input = settled(short_k * short_v)
    short_mix = causal_apply(short_input, taps_block, total, SEQ)
    hidden = settled(short_q * short_mix)
    long_input = settled(long_k * hidden)
    times = jnp.arange(SEQ, dtype=jnp.float32)[:, None]
    long_filter = jnp.zeros((SEQ, taps_block.shape[1]), jnp.float32)
    for mode_index in range(MODES):
        long_filter = long_filter + residue_block[mode_index][None, :] * jnp.exp(-rate_block[mode_index][None, :] * times)
    long_mix = causal_apply(long_input, long_filter, total, SEQ)
    core_output = (long_q * long_mix).astype(jnp.bfloat16)
    query_long_grad = (upstream * long_mix).astype(jnp.bfloat16)
    long_back = upstream * long_q
    long_input_grad = settled(correlate(long_back, long_filter, total, SEQ))
    key_long_grad = (long_input_grad * hidden).astype(jnp.bfloat16)
    hidden_grad = long_input_grad * long_k
    query_short_grad = (hidden_grad * short_mix).astype(jnp.bfloat16)
    short_back = settled(hidden_grad * short_q)
    short_input_grad = correlate(short_back, taps_block, total, SEQ)
    key_short_grad = (short_input_grad * short_v).astype(jnp.bfloat16)
    value_short_grad = (short_input_grad * short_k).astype(jnp.bfloat16)
    taps_grad = correlate(short_back, short_input, total, MR_LEN) * (SEQ ** -0.5)
    return (core_output, query_short_grad, key_short_grad, value_short_grad, query_long_grad, key_long_grad, taps_grad.astype(jnp.float32))


def reference(query_short, key_short, value_short, short_taps, query_long, key_long, long_residue, long_rate, cotangent):
    block_width = 256
    count = D // block_width

    def split(array):
        return array.reshape(array.shape[0], count, block_width).transpose(1, 0, 2)

    def merge(array):
        return array.transpose(1, 0, 2).reshape(array.shape[1], D)

    pieces = (split(query_short), split(key_short), split(value_short), split(short_taps), split(query_long), split(key_long), split(long_residue), split(long_rate), split(cotangent))
    results = lax.map(channel_block, pieces)
    return (merge(results[0]), merge(results[1]), merge(results[2]), merge(results[3]), merge(results[4]), merge(results[5]), merge(results[6]))
```

```python
import functools
import math

import jax
import jax.numpy as jnp
import ml_dtypes
import numpy as np
from jax import lax
from jax.experimental import pallas as pl
from jax.experimental.pallas import tpu as pltpu
from jax.sharding import PartitionSpec as P

F32 = jnp.float32
BF16 = jnp.bfloat16
T = 128
N = 2 * T
MG = 4
LANES = 128
VMEM_LIMIT = 56 * 1024 * 1024


def forward_table():
    n = np.arange(N)
    k = np.arange(T)
    angle = 2.0 * np.pi * ((k[:, None] * n[None, :]) % N) / N
    low = -np.sin(angle)
    low[0] = (-1.0) ** n
    return np.concatenate([np.cos(angle), low], axis=0)


def inverse_table(rows):
    n = np.asarray(rows)
    k = np.arange(T)
    angle = 2.0 * np.pi * ((n[:, None] * k[None, :]) % N) / N
    weight = np.full((T,), 2.0 / N)
    weight[0] = 1.0 / N
    low = -np.sin(angle) * weight
    low[:, 0] = (-1.0) ** n / N
    return np.concatenate([np.cos(angle) * weight, low], axis=1)


def halves(table):
    high = table.astype(ml_dtypes.bfloat16)
    low = (table - high.astype(np.float64)).astype(ml_dtypes.bfloat16)
    return high, low


def two_terms(table):
    high, low = halves(table)
    return np.concatenate([high, low], axis=1)


def three_terms(table):
    high, low = halves(table)
    return np.concatenate([high, low, high], axis=1)


def dot(table, data):
    return jnp.dot(table, data, preferred_element_type=F32)


def exact(data):
    return jnp.concatenate([data, data], axis=0)


def split(data):
    high = data.astype(BF16)
    low = (data - high.astype(F32)).astype(BF16)
    return jnp.concatenate([high, high, low], axis=0)


def product(first, second, conjugate):
    ar, ai = first[:T], first[T:]
    br, bi = second[:T], second[T:]
    top = lax.broadcasted_iota(jnp.int32, ar.shape, 0) == 0
    rr, ii = ar * br, ai * bi
    if conjugate:
        re = rr + jnp.where(top, 0.0, ii)
        im = jnp.where(top, ii, ai * br - ar * bi)
    else:
        re = rr - jnp.where(top, 0.0, ii)
        im = jnp.where(top, ii, ai * br + ar * bi)
    return jnp.concatenate([re, im], axis=0)


def rows_iota():
    return lax.broadcasted_iota(jnp.int32, (8, LANES), 0).astype(F32)


def state_sums(data, rate, first_power, newest_last):
    iota = rows_iota()
    powers = (7.0 - iota) if newest_last else iota
    order = range(T // 8) if newest_last else range(T // 8 - 1, -1, -1)
    tiles = [data[8 * q : 8 * q + 8] for q in order]
    rows = []
    for m in range(rate.shape[0]):
        a = rate[m : m + 1]
        step = jnp.broadcast_to(jnp.exp(-8.0 * a), (8, LANES))
        total = tiles[0]
        for tile in tiles[1:]:
            total = total * step + tile
        rows.append(jnp.sum(total * jnp.exp(-a * powers), axis=0, keepdims=True))
    return rows


def mode_series(out_ref, lanes, scales, rate, powers, rising):
    steps, terms = [], []
    for m in range(rate.shape[0]):
        a = rate[m : m + 1]
        steps.append(jnp.broadcast_to(jnp.exp(-8.0 * a), (8, LANES)))
        terms.append(scales[m] * jnp.exp(-a * powers))
    order = range(T // 8) if rising else range(T // 8 - 1, -1, -1)
    for place, q in enumerate(order):
        if place:
            terms = [term * step for term, step in zip(terms, steps)]
        layer = terms
        while len(layer) > 1:
            layer = [layer[i] + layer[i + 1] for i in range(0, len(layer), 2)]
        out_ref[8 * q : 8 * q + 8, lanes] = layer[0]


def put_states(out_ref, group, rows):
    for m, row in enumerate(rows):
        out_ref[m // MG, group, m % MG : m % MG + 1, :] = row


def back_states_kernel(query_ref, cot_ref, rate_ref, out_ref):
    for group in range(query_ref.shape[1] // LANES):
        lanes = pl.ds(group * LANES, LANES)
        back = query_ref[:, lanes].astype(F32) * cot_ref[:, lanes].astype(F32)
        put_states(out_ref, group, state_sums(back, rate_ref[:, lanes], 0, False))


def take_scales(states_ref, group, residue):
    return [
        residue[m : m + 1] * states_ref[m // MG, group, m % MG : m % MG + 1, :]
        for m in range(residue.shape[0])
    ]


def long_back_kernel(
    query_ref,
    cot_ref,
    key_ref,
    short_query_ref,
    residue_ref,
    rate_ref,
    states_ref,
    forward3_ref,
    inverse_ref,
    grad_ref,
    short_back_ref,
    filter_ref,
    taps_scr,
    carry_scr,
):
    iota = rows_iota()
    for group in range(query_ref.shape[1] // LANES):
        lanes = pl.ds(group * LANES, LANES)
        rate, residue = rate_ref[:, lanes], residue_ref[:, lanes]
        scales = [residue[m : m + 1] for m in range(rate.shape[0])]
        mode_series(taps_scr, lanes, scales, rate, iota, True)
        mode_series(
            carry_scr, lanes, take_scales(states_ref, group, residue), rate, 8.0 - iota, False
        )
    spectrum = dot(forward3_ref[...], split(taps_scr[...]))
    filter_ref[...] = spectrum
    back = query_ref[...].astype(F32) * cot_ref[...].astype(F32)
    turned = product(dot(forward3_ref[...], split(back)), spectrum, True)
    grad = (dot(inverse_ref[...], split(turned)) + carry_scr[...]).astype(BF16)
    grad_ref[...] = grad
    hidden_grad = grad.astype(F32) * key_ref[...].astype(F32)
    short_back_ref[...] = (hidden_grad * short_query_ref[...].astype(F32)).astype(BF16)


def short_front_kernel(
    short_input_ref,
    front_ref,
    taps_ref,
    short_query_ref,
    key_ref,
    grad_ref,
    short_back_ref,
    rate_ref,
    forward_ref,
    forward2_ref,
    forward3_ref,
    inverse_mix_ref,
    inverse_taps_ref,
    query_grad_ref,
    key_grad_ref,
    long_input_ref,
    states_ref,
    taps_spec_ref,
    lag_ref,
    input_scr,
):
    extended = jnp.concatenate([front_ref[...], short_input_ref[...]], axis=0)
    spectrum = dot(forward_ref[...], exact(extended))
    taps_spec = dot(forward3_ref[...], split(taps_ref[...]))
    taps_spec_ref[...] = taps_spec
    short_mix = dot(inverse_mix_ref[...], split(product(spectrum, taps_spec, False)))
    hidden = (short_query_ref[...].astype(F32) * short_mix).astype(BF16).astype(F32)
    key = key_ref[...].astype(F32)
    grad = grad_ref[...].astype(F32)
    key_grad_ref[...] = (grad * hidden).astype(BF16)
    query_grad_ref[...] = (grad * key * short_mix).astype(BF16)
    long_input = (key * hidden).astype(BF16)
    long_input_ref[...] = long_input
    input_scr[...] = long_input.astype(F32)
    for group in range(rate_ref.shape[1] // LANES):
        lanes = pl.ds(group * LANES, LANES)
        put_states(
            states_ref, group, state_sums(input_scr[:, lanes], rate_ref[:, lanes], 0, True)
        )
    own = dot(forward2_ref[...], exact(short_back_ref[...]))
    lag = dot(inverse_taps_ref[...], split(product(spectrum, own, True)))
    lag_ref[...] = lag.reshape(lag_ref.shape)


def rear_kernel(
    long_input_ref,
    filter_ref,
    states_ref,
    residue_ref,
    rate_ref,
    query_ref,
    cot_ref,
    short_back_ref,
    behind_ref,
    taps_spec_ref,
    short_key_ref,
    value_ref,
    forward_ref,
    forward2_ref,
    inverse_ref,
    core_ref,
    gate_grad_ref,
    key_grad_ref,
    value_grad_ref,
    carry_scr,
):
    iota = rows_iota()
    for group in range(query_ref.shape[1] // LANES):
        lanes = pl.ds(group * LANES, LANES)
        rate, residue = rate_ref[:, lanes], residue_ref[:, lanes]
        mode_series(
            carry_scr, lanes, take_scales(states_ref, group, residue), rate, iota + 1.0, True
        )
    spectrum = dot(forward2_ref[...], exact(long_input_ref[...]))
    turned = product(spectrum, filter_ref[...], False)
    long_mix = dot(inverse_ref[...], split(turned)) + carry_scr[...]
    core_ref[...] = (query_ref[...].astype(F32) * long_mix).astype(BF16)
    gate_grad_ref[...] = (cot_ref[...].astype(F32) * long_mix).astype(BF16)
    extended = jnp.concatenate([short_back_ref[...], behind_ref[...]], axis=0)
    back = dot(forward_ref[...], exact(extended))
    input_grad = dot(inverse_ref[...], split(product(back, taps_spec_ref[...], True)))
    key_grad_ref[...] = (input_grad * value_ref[...].astype(F32)).astype(BF16)
    value_grad_ref[...] = (input_grad * short_key_ref[...].astype(F32)).astype(BF16)


def scan_kernel(pieces_ref, rate_ref, out_ref, *, reverse):
    count = pieces_ref.shape[0]
    step = jnp.exp(-float(T) * rate_ref[...])
    carry = jnp.zeros(step.shape, F32)
    order = range(count - 1, -1, -1) if reverse else range(count)
    for i in order:
        out_ref[i] = carry
        carry = carry * step + pieces_ref[i]


def scan_states(pieces, rate_piece, reverse):
    return pl.pallas_call(
        functools.partial(scan_kernel, reverse=reverse),
        out_shape=jax.ShapeDtypeStruct(pieces.shape, F32),
        compiler_params=pltpu.CompilerParams(vmem_limit_bytes=VMEM_LIMIT),
    )(pieces, rate_piece)


def exchange(pieces):
    return lax.all_to_all(pieces, "ctx", split_axis=0, concat_axis=0, tiled=True)


def passed_along(block, distance):
    devices = range(lax.axis_size("ctx"))
    route = [(i - distance, i) for i in devices if i - distance in devices]
    return lax.ppermute(block, "ctx", route)


def over_blocks(kernel, width, channels, arrays, outs, scratch, flops):
    kinds = {
        "col": lambda shape: pl.BlockSpec((shape[0], width), lambda i: (0, i)),
        "all": lambda shape: pl.BlockSpec(shape, lambda i: (0,) * len(shape)),
        "state": lambda shape: pl.BlockSpec(
            (shape[0], width // LANES) + shape[2:], lambda i: (0, i, 0, 0)
        ),
        "lag": lambda shape: pl.BlockSpec((shape[0], 1) + shape[2:], lambda i: (0, i, 0, 0)),
    }
    moved = sum(a.size * a.dtype.itemsize for _, a in arrays)
    moved += sum(math.prod(s) * jnp.dtype(d).itemsize for _, s, d in outs)
    return pl.pallas_call(
        kernel,
        grid=(channels // width,),
        in_specs=[kinds[kind](a.shape) for kind, a in arrays],
        out_specs=[kinds[kind](shape) for kind, shape, _ in outs],
        out_shape=[jax.ShapeDtypeStruct(shape, dtype) for _, shape, dtype in outs],
        scratch_shapes=scratch,
        compiler_params=pltpu.CompilerParams(vmem_limit_bytes=VMEM_LIMIT),
        cost_estimate=pl.CostEstimate(flops=flops, bytes_accessed=moved, transcendentals=0),
    )(*[a for _, a in arrays])


def local(
    query_short,
    key_short,
    value_short,
    short_taps,
    query_long,
    key_long,
    long_residue,
    long_rate,
    cotangent,
):
    groups = lax.axis_size("ctx")
    tokens_here, channels = query_short.shape
    modes = long_rate.shape[0]
    sequence = tokens_here * groups
    width = 512
    lane_groups = channels // LANES
    state_shape = (modes // MG, lane_groups, MG, LANES)
    piece_shape = (groups, MG, LANES)

    forward = forward_table()
    forward_full = jnp.asarray(two_terms(forward))
    forward_two = jnp.asarray(two_terms(forward[:, :T]))
    forward_three = jnp.asarray(three_terms(forward[:, :T]))
    inverse_low = jnp.asarray(three_terms(inverse_table(np.arange(T))))
    inverse_high = jnp.asarray(three_terms(inverse_table(np.arange(T) + T)))
    inverse_lags = jnp.asarray(three_terms(inverse_table(T - np.arange(T))))

    me = lax.axis_index("ctx")
    rate_piece = lax.dynamic_slice(
        long_rate, (me // lane_groups * MG, me % lane_groups * LANES), (MG, LANES)
    )

    short_input = (key_short.astype(F32) * value_short.astype(F32)).astype(BF16)
    front = passed_along(short_input, 1)

    col = (tokens_here, channels)
    (back_states,) = over_blocks(
        back_states_kernel,
        width,
        channels,
        [("col", query_long), ("col", cotangent), ("col", long_rate)],
        [("state", state_shape, F32)],
        [],
        10**10,
    )
    later = exchange(
        scan_states(exchange(back_states.reshape(piece_shape)), rate_piece, True)
    ).reshape(state_shape)
    grad, short_back, filter_spec = over_blocks(
        long_back_kernel,
        width,
        channels,
        [
            ("col", query_long),
            ("col", cotangent),
            ("col", key_long),
            ("col", query_short),
            ("col", long_residue),
            ("col", long_rate),
            ("state", later),
            ("all", forward_three),
            ("all", inverse_low),
        ],
        [("col", col, BF16), ("col", col, BF16), ("col", (N, channels), F32)],
        [pltpu.VMEM((T, width), F32), pltpu.VMEM((T, width), F32)],
        10**10,
    )
    behind = passed_along(short_back, -1)
    lag_shape = (T // 8, channels // width, 8, width)
    query_short_grad, key_long_grad, long_input, states, taps_spec, lags = over_blocks(
        short_front_kernel,
        width,
        channels,
        [
            ("col", short_input),
            ("col", front),
            ("col", short_taps),
            ("col", query_short),
            ("col", key_long),
            ("col", grad),
            ("col", short_back),
            ("col", long_rate),
            ("all", forward_full),
            ("all", forward_two),
            ("all", forward_three),
            ("all", inverse_high),
            ("all", inverse_lags),
        ],
        [
            ("col", col, BF16),
            ("col", col, BF16),
            ("col", col, BF16),
            ("state", state_shape, F32),
            ("col", (N, channels), F32),
            ("lag", lag_shape, F32),
        ],
        [pltpu.VMEM((T, width), F32)],
        10**10,
    )
    earlier = exchange(
        scan_states(exchange(states.reshape(piece_shape)), rate_piece, False)
    ).reshape(state_shape)
    core_output, query_long_grad, key_short_grad, value_short_grad = over_blocks(
        rear_kernel,
        width,
        channels,
        [
            ("col", long_input),
            ("col", filter_spec),
            ("state", earlier),
            ("col", long_residue),
            ("col", long_rate),
            ("col", query_long),
            ("col", cotangent),
            ("col", short_back),
            ("col", behind),
            ("col", taps_spec),
            ("col", key_short),
            ("col", value_short),
            ("all", forward_full),
            ("all", forward_two),
            ("all", inverse_low),
        ],
        [("col", col, BF16)] * 4,
        [pltpu.VMEM((T, width), F32)],
        10**10,
    )
    lag_pieces = exchange(lags.reshape((groups, 8, width)))
    own_lags = jnp.sum(lag_pieces, axis=0) * (sequence**-0.5)
    all_lags = exchange(jnp.broadcast_to(own_lags[None], (groups, 8, width)))
    taps_grad = (
        all_lags.reshape(lag_shape).transpose(0, 2, 1, 3).reshape(short_taps.shape)
    )
    return (
        core_output,
        query_short_grad,
        key_short_grad,
        value_short_grad,
        query_long_grad,
        key_long_grad,
        taps_grad,
    )


def solution(mesh):
    tokens = P("ctx", "ch")
    table = P(None, "ch")
    return jax.shard_map(
        local,
        mesh=mesh,
        in_specs=(tokens, tokens, tokens, table, tokens, tokens, table, table, tokens),
        out_specs=(tokens, tokens, tokens, tokens, tokens, tokens, table),
        check_vma=False,
    )
```

```python
import functools

import jax
import jax.numpy as jnp
import ml_dtypes
import numpy as np
from jax import lax
from jax.experimental import pallas as pl
from jax.experimental.pallas import tpu as pltpu
from jax.sharding import PartitionSpec as P

F32 = jnp.float32
BF16 = jnp.bfloat16
T = 128
N = 2 * T
MG = 4
LANES = 128
VMEM_LIMIT = 56 * 1024 * 1024
PLANE_X = 4
MESH = pl.DeviceIdType.MESH
COST = pl.CostEstimate(flops=10**6, bytes_accessed=2**16, transcendentals=0)


def forward_table():
    n = np.arange(N)
    k = np.arange(T)
    angle = 2.0 * np.pi * ((k[:, None] * n[None, :]) % N) / N
    low = -np.sin(angle)
    low[0] = (-1.0) ** n
    return np.concatenate([np.cos(angle), low], axis=0)


def inverse_table(rows):
    n = np.asarray(rows)
    k = np.arange(T)
    angle = 2.0 * np.pi * ((n[:, None] * k[None, :]) % N) / N
    weight = np.full((T,), 2.0 / N)
    weight[0] = 1.0 / N
    low = -np.sin(angle) * weight
    low[:, 0] = (-1.0) ** n / N
    return np.concatenate([np.cos(angle) * weight, low], axis=1)


def halves(table):
    high = table.astype(ml_dtypes.bfloat16)
    low = (table - high.astype(np.float64)).astype(ml_dtypes.bfloat16)
    return high, low


def two_terms(table):
    high, low = halves(table)
    return np.concatenate([high, low], axis=1)


def three_terms(table):
    high, low = halves(table)
    return np.concatenate([high, low, high], axis=1)


def dot(table, data):
    return jnp.dot(table, data, preferred_element_type=F32)


def exact(data):
    return jnp.concatenate([data, data], axis=0)


def split(data):
    high = data.astype(BF16)
    low = (data - high.astype(F32)).astype(BF16)
    return jnp.concatenate([high, high, low], axis=0)


def product(first, second, conjugate):
    ar, ai = first[:T], first[T:]
    br, bi = second[:T], second[T:]
    top = lax.broadcasted_iota(jnp.int32, ar.shape, 0) == 0
    rr, ii = ar * br, ai * bi
    if conjugate:
        re = rr + jnp.where(top, 0.0, ii)
        im = jnp.where(top, ii, ai * br - ar * bi)
    else:
        re = rr - jnp.where(top, 0.0, ii)
        im = jnp.where(top, ii, ai * br + ar * bi)
    return jnp.concatenate([re, im], axis=0)


def rows_iota():
    return lax.broadcasted_iota(jnp.int32, (8, LANES), 0).astype(F32)


def state_sums(data, rate, first_power, newest_last):
    iota = rows_iota()
    powers = (7.0 - iota) if newest_last else iota
    order = range(T // 8) if newest_last else range(T // 8 - 1, -1, -1)
    tiles = [data[8 * q : 8 * q + 8] for q in order]
    rows = []
    for m in range(rate.shape[0]):
        a = rate[m : m + 1]
        step = jnp.broadcast_to(jnp.exp(-8.0 * a), (8, LANES))
        total = tiles[0]
        for tile in tiles[1:]:
            total = total * step + tile
        rows.append(jnp.sum(total * jnp.exp(-a * powers), axis=0, keepdims=True))
    return rows


def mode_series(out_ref, lanes, scales, rate, powers, rising):
    steps, terms = [], []
    for m in range(rate.shape[0]):
        a = rate[m : m + 1]
        steps.append(jnp.broadcast_to(jnp.exp(-8.0 * a), (8, LANES)))
        terms.append(scales[m] * jnp.exp(-a * powers))
    order = range(T // 8) if rising else range(T // 8 - 1, -1, -1)
    for place, q in enumerate(order):
        if place:
            terms = [term * step for term, step in zip(terms, steps)]
        layer = terms
        while len(layer) > 1:
            layer = [layer[i] + layer[i + 1] for i in range(0, len(layer), 2)]
        out_ref[8 * q : 8 * q + 8, lanes] = layer[0]


def put_states(out_ref, group, rows):
    for m, row in enumerate(rows):
        out_ref[m // MG, group, m % MG : m % MG + 1, :] = row


def back_states_kernel(query_ref, cot_ref, rate_ref, out_ref):
    for group in range(query_ref.shape[1] // LANES):
        lanes = pl.ds(group * LANES, LANES)
        back = query_ref[:, lanes].astype(F32) * cot_ref[:, lanes].astype(F32)
        put_states(out_ref, group, state_sums(back, rate_ref[:, lanes], 0, False))


def take_scales(states_ref, group, residue):
    return [
        residue[m : m + 1] * states_ref[m // MG, group, m % MG : m % MG + 1, :]
        for m in range(residue.shape[0])
    ]


def long_back_kernel(
    query_ref,
    cot_ref,
    key_ref,
    short_query_ref,
    residue_ref,
    rate_ref,
    states_ref,
    forward3_ref,
    inverse_ref,
    grad_ref,
    short_back_ref,
    filter_ref,
    taps_scr,
    carry_scr,
):
    iota = rows_iota()
    for group in range(query_ref.shape[1] // LANES):
        lanes = pl.ds(group * LANES, LANES)
        rate, residue = rate_ref[:, lanes], residue_ref[:, lanes]
        scales = [residue[m : m + 1] for m in range(rate.shape[0])]
        mode_series(taps_scr, lanes, scales, rate, iota, True)
        mode_series(
            carry_scr, lanes, take_scales(states_ref, group, residue), rate, 8.0 - iota, False
        )
    spectrum = dot(forward3_ref[...], split(taps_scr[...]))
    filter_ref[...] = spectrum
    back = query_ref[...].astype(F32) * cot_ref[...].astype(F32)
    turned = product(dot(forward3_ref[...], split(back)), spectrum, True)
    grad = (dot(inverse_ref[...], split(turned)) + carry_scr[...]).astype(BF16)
    grad_ref[...] = grad
    hidden_grad = grad.astype(F32) * key_ref[...].astype(F32)
    short_back_ref[...] = (hidden_grad * short_query_ref[...].astype(F32)).astype(BF16)


def short_front_kernel(
    short_input_ref,
    front_ref,
    taps_ref,
    short_query_ref,
    key_ref,
    grad_ref,
    short_back_ref,
    rate_ref,
    forward_ref,
    forward2_ref,
    forward3_ref,
    inverse_mix_ref,
    inverse_taps_ref,
    query_grad_ref,
    key_grad_ref,
    long_input_ref,
    states_ref,
    taps_spec_ref,
    lag_ref,
    input_scr,
):
    extended = jnp.concatenate([front_ref[...], short_input_ref[...]], axis=0)
    spectrum = dot(forward_ref[...], exact(extended))
    taps_spec = dot(forward3_ref[...], split(taps_ref[...]))
    taps_spec_ref[...] = taps_spec
    short_mix = dot(inverse_mix_ref[...], split(product(spectrum, taps_spec, False)))
    hidden = (short_query_ref[...].astype(F32) * short_mix).astype(BF16).astype(F32)
    key = key_ref[...].astype(F32)
    grad = grad_ref[...].astype(F32)
    key_grad_ref[...] = (grad * hidden).astype(BF16)
    query_grad_ref[...] = (grad * key * short_mix).astype(BF16)
    long_input = (key * hidden).astype(BF16)
    long_input_ref[...] = long_input
    input_scr[...] = long_input.astype(F32)
    for group in range(rate_ref.shape[1] // LANES):
        lanes = pl.ds(group * LANES, LANES)
        put_states(
            states_ref, group, state_sums(input_scr[:, lanes], rate_ref[:, lanes], 0, True)
        )
    own = dot(forward2_ref[...], exact(short_back_ref[...]))
    lag = dot(inverse_taps_ref[...], split(product(spectrum, own, True)))
    lag_ref[...] = lag


def rear_kernel(
    long_input_ref,
    filter_ref,
    states_ref,
    residue_ref,
    rate_ref,
    query_ref,
    cot_ref,
    short_back_ref,
    behind_ref,
    taps_spec_ref,
    short_key_ref,
    value_ref,
    forward_ref,
    forward2_ref,
    inverse_ref,
    core_ref,
    gate_grad_ref,
    key_grad_ref,
    value_grad_ref,
    carry_scr,
):
    iota = rows_iota()
    for group in range(query_ref.shape[1] // LANES):
        lanes = pl.ds(group * LANES, LANES)
        rate, residue = rate_ref[:, lanes], residue_ref[:, lanes]
        mode_series(
            carry_scr, lanes, take_scales(states_ref, group, residue), rate, iota + 1.0, True
        )
    spectrum = dot(forward2_ref[...], exact(long_input_ref[...]))
    turned = product(spectrum, filter_ref[...], False)
    long_mix = dot(inverse_ref[...], split(turned)) + carry_scr[...]
    core_ref[...] = (query_ref[...].astype(F32) * long_mix).astype(BF16)
    gate_grad_ref[...] = (cot_ref[...].astype(F32) * long_mix).astype(BF16)
    extended = jnp.concatenate([short_back_ref[...], behind_ref[...]], axis=0)
    back = dot(forward_ref[...], exact(extended))
    input_grad = dot(inverse_ref[...], split(product(back, taps_spec_ref[...], True)))
    key_grad_ref[...] = (input_grad * value_ref[...].astype(F32)).astype(BF16)
    value_grad_ref[...] = (input_grad * short_key_ref[...].astype(F32)).astype(BF16)


def peer_loop(count, body):
    lax.fori_loop(1, count, lambda i, _: (body(i), 0)[1], 0)


def greet(me, count):
    barrier = pltpu.get_barrier_semaphore()

    def signal(i):
        pl.semaphore_signal(
            barrier, inc=1, device_id={"ctx": lax.rem(me + i, count)}, device_id_type=MESH
        )

    peer_loop(count, signal)
    pl.semaphore_wait(barrier, count - 1)


def send(source, target, peer, send_sem, recv_sem):
    copy = pltpu.make_async_remote_copy(
        src_ref=source,
        dst_ref=target,
        send_sem=send_sem,
        recv_sem=recv_sem,
        device_id={"ctx": peer},
        device_id_type=MESH,
    )
    copy.start()
    return copy


def wait_bytes(ref, sem):
    pltpu.make_async_copy(ref, ref, sem).wait()


def spread(source_ref, target_ref, me, count, send_sem, recv_sem):
    def body(i):
        peer = lax.rem(me + i, count)
        send(source_ref.at[peer], target_ref.at[me], peer, send_sem, recv_sem)

    peer_loop(count, body)
    target_ref[me] = source_ref[me]


def scan_pieces(pieces_ref, carries_ref, rate_ref, reverse):
    count = pieces_ref.shape[0]
    step = jnp.exp(-float(T) * rate_ref[...])

    def body(i, carry):
        place = count - 1 - i if reverse else i
        carries_ref[place] = carry
        return carry * step + pieces_ref[place]

    lax.fori_loop(0, count, body, jnp.zeros(step.shape, F32))


def states_kernel(
    states_ref, rate_ref, out_ref, pieces_scr, carries_scr, send_sems, recv_sems, *, reverse
):
    count = states_ref.shape[0]
    me = lax.axis_index("ctx")
    others = pl.ds(0, count - 1)
    greet(me, count)
    spread(states_ref, pieces_scr, me, count, send_sems.at[0], recv_sems.at[0])
    wait_bytes(pieces_scr.at[others], recv_sems.at[0])
    scan_pieces(pieces_scr, carries_scr, rate_ref, reverse)
    spread(carries_scr, out_ref, me, count, send_sems.at[1], recv_sems.at[1])
    wait_bytes(out_ref.at[others], recv_sems.at[1])
    wait_bytes(states_ref.at[others], send_sems.at[0])
    wait_bytes(carries_scr.at[others], send_sems.at[1])


def states_and_lags_kernel(
    states_ref,
    rate_ref,
    lags_ref,
    out_ref,
    taps_ref,
    pieces_scr,
    carries_scr,
    half_scr,
    sum_scr,
    plane_scr,
    own_scr,
    pair_scr,
    send_sems,
    recv_sems,
    *,
    scale,
):
    count = states_ref.shape[0]
    me = lax.axis_index("ctx")
    others = pl.ds(0, count - 1)
    core = lax.rem(me, 2)
    along_x = lax.rem(me // 2, PLANE_X)
    far = lax.rem(me // (2 * PLANE_X), 2)
    along_y = me // (4 * PLANE_X)
    planes = count // 4
    spot = along_y * PLANE_X + along_x
    sibling = me + 1 - 2 * core
    partner = me + 2 * PLANE_X * (1 - 2 * far)
    width = lags_ref.shape[1] // 2
    mine = pl.ds(pl.multiple_of(core * width, LANES), width)
    theirs = pl.ds(pl.multiple_of((1 - core) * width, LANES), width)

    def device_at(place):
        return (place // PLANE_X * 2 + far) * 2 * PLANE_X + lax.rem(place, PLANE_X) * 2 + core

    def rows(place):
        return pl.ds(pl.multiple_of(place * 8, 8), 8)

    greet(me, count)
    spread(states_ref, pieces_scr, me, count, send_sems.at[0], recv_sems.at[0])
    first = send(lags_ref.at[:, theirs], half_scr, sibling, send_sems.at[2], recv_sems.at[2])
    wait_bytes(pieces_scr.at[others], recv_sems.at[0])
    scan_pieces(pieces_scr, carries_scr, rate_ref, False)
    spread(carries_scr, out_ref, me, count, send_sems.at[1], recv_sems.at[1])

    first.wait()
    sum_scr[...] = (lags_ref[:, mine] + half_scr[...]).reshape(sum_scr.shape)

    def to_plane(i):
        place = lax.rem(spot + i, planes)
        send(
            sum_scr.at[place],
            plane_scr.at[spot],
            device_at(place),
            send_sems.at[3],
            recv_sems.at[3],
        )

    peer_loop(planes, to_plane)
    plane_scr[spot] = sum_scr[spot]
    wait_bytes(plane_scr.at[pl.ds(0, planes - 1)], recv_sems.at[3])
    total = plane_scr[0]
    for place in range(1, planes):
        total = total + plane_scr[place]
    own_scr[...] = total
    second = send(own_scr, pair_scr, partner, send_sems.at[4], recv_sems.at[4])
    second.wait()
    own_scr[...] = (own_scr[...] + pair_scr[...]) * scale

    def from_plane(i):
        place = lax.rem(spot + i, planes)
        send(
            own_scr,
            taps_ref.at[rows(spot), mine],
            device_at(place),
            send_sems.at[5],
            recv_sems.at[5],
        )

    peer_loop(planes, from_plane)
    taps_ref[rows(spot), mine] = own_scr[...]
    wait_bytes(plane_scr.at[pl.ds(0, planes - 1)], recv_sems.at[5])
    last = send(
        taps_ref.at[:, mine], taps_ref.at[:, mine], sibling, send_sems.at[6], recv_sems.at[6]
    )
    last.wait()
    wait_bytes(out_ref.at[others], recv_sems.at[1])
    wait_bytes(states_ref.at[others], send_sems.at[0])
    wait_bytes(carries_scr.at[others], send_sems.at[1])
    wait_bytes(sum_scr.at[pl.ds(0, planes - 1)], send_sems.at[3])
    wait_bytes(sum_scr.at[pl.ds(0, planes - 1)], send_sems.at[5])


def whole(shape, dtype):
    return pltpu.VMEM(shape, dtype)


def exchange_states(states, rate_piece, reverse):
    return pl.pallas_call(
        functools.partial(states_kernel, reverse=reverse),
        out_shape=jax.ShapeDtypeStruct(states.shape, F32),
        in_specs=[pl.BlockSpec(memory_space=pltpu.VMEM)] * 2,
        out_specs=pl.BlockSpec(memory_space=pltpu.VMEM),
        scratch_shapes=[
            whole(states.shape, F32),
            whole(states.shape, F32),
            pltpu.SemaphoreType.DMA((2,)),
            pltpu.SemaphoreType.DMA((2,)),
        ],
        compiler_params=pltpu.CompilerParams(
            collective_id=0, has_side_effects=True, vmem_limit_bytes=VMEM_LIMIT
        ),
        cost_estimate=COST,
    )(states, rate_piece)


def exchange_states_and_lags(states, rate_piece, lags, scale):
    rows, channels = lags.shape
    width = channels // 2
    planes = states.shape[0] // 4
    return pl.pallas_call(
        functools.partial(states_and_lags_kernel, scale=scale),
        out_shape=[
            jax.ShapeDtypeStruct(states.shape, F32),
            jax.ShapeDtypeStruct(lags.shape, F32),
        ],
        in_specs=[pl.BlockSpec(memory_space=pltpu.VMEM)] * 3,
        out_specs=[pl.BlockSpec(memory_space=pltpu.VMEM)] * 2,
        scratch_shapes=[
            whole(states.shape, F32),
            whole(states.shape, F32),
            whole((rows, width), F32),
            whole((planes, rows // planes, width), F32),
            whole((planes, rows // planes, width), F32),
            whole((rows // planes, width), F32),
            whole((rows // planes, width), F32),
            pltpu.SemaphoreType.DMA((7,)),
            pltpu.SemaphoreType.DMA((7,)),
        ],
        compiler_params=pltpu.CompilerParams(
            collective_id=1, has_side_effects=True, vmem_limit_bytes=VMEM_LIMIT
        ),
        cost_estimate=COST,
    )(states, rate_piece, lags)


def passed_along(block, distance):
    devices = range(lax.axis_size("ctx"))
    route = [(i - distance, i) for i in devices if i - distance in devices]
    return lax.ppermute(block, "ctx", route)


def over_blocks(kernel, width, channels, arrays, outs, scratch, flops):
    kinds = {
        "col": lambda shape: pl.BlockSpec((shape[0], width), lambda i: (0, i)),
        "all": lambda shape: pl.BlockSpec(shape, lambda i: (0,) * len(shape)),
        "state": lambda shape: pl.BlockSpec(
            (shape[0], width // LANES) + shape[2:], lambda i: (0, i, 0, 0)
        ),
    }
    return pl.pallas_call(
        kernel,
        grid=(channels // width,),
        in_specs=[kinds[kind](a.shape) for kind, a in arrays],
        out_specs=[kinds[kind](shape) for kind, shape, _ in outs],
        out_shape=[jax.ShapeDtypeStruct(shape, dtype) for _, shape, dtype in outs],
        scratch_shapes=scratch,
        compiler_params=pltpu.CompilerParams(vmem_limit_bytes=VMEM_LIMIT),
        cost_estimate=pl.CostEstimate(flops=flops, bytes_accessed=2**16, transcendentals=0),
    )(*[a for _, a in arrays])


def local(
    query_short,
    key_short,
    value_short,
    short_taps,
    query_long,
    key_long,
    long_residue,
    long_rate,
    cotangent,
):
    groups = lax.axis_size("ctx")
    tokens_here, channels = query_short.shape
    modes = long_rate.shape[0]
    sequence = tokens_here * groups
    width = 512
    lane_groups = channels // LANES
    state_shape = (modes // MG, lane_groups, MG, LANES)
    piece_shape = (groups, MG, LANES)

    forward = forward_table()
    forward_full = jnp.asarray(two_terms(forward))
    forward_two = jnp.asarray(two_terms(forward[:, :T]))
    forward_three = jnp.asarray(three_terms(forward[:, :T]))
    inverse_low = jnp.asarray(three_terms(inverse_table(np.arange(T))))
    inverse_high = jnp.asarray(three_terms(inverse_table(np.arange(T) + T)))
    inverse_lags = jnp.asarray(three_terms(inverse_table(T - np.arange(T))))

    me = lax.axis_index("ctx")
    rate_piece = lax.dynamic_slice(
        long_rate, (me // lane_groups * MG, me % lane_groups * LANES), (MG, LANES)
    )

    short_input = (key_short.astype(F32) * value_short.astype(F32)).astype(BF16)
    front = passed_along(short_input, 1)

    col = (tokens_here, channels)
    (back_states,) = over_blocks(
        back_states_kernel,
        width,
        channels,
        [("col", query_long), ("col", cotangent), ("col", long_rate)],
        [("state", state_shape, F32)],
        [],
        10**6,
    )
    later = exchange_states(back_states.reshape(piece_shape), rate_piece, True)
    later = later.reshape(state_shape)
    grad, short_back, filter_spec = over_blocks(
        long_back_kernel,
        width,
        channels,
        [
            ("col", query_long),
            ("col", cotangent),
            ("col", key_long),
            ("col", query_short),
            ("col", long_residue),
            ("col", long_rate),
            ("state", later),
            ("all", forward_three),
            ("all", inverse_low),
        ],
        [("col", col, BF16), ("col", col, BF16), ("col", (N, channels), F32)],
        [pltpu.VMEM((T, width), F32), pltpu.VMEM((T, width), F32)],
        10**6,
    )
    behind = passed_along(short_back, -1)
    query_short_grad, key_long_grad, long_input, states, taps_spec, lags = over_blocks(
        short_front_kernel,
        width,
        channels,
        [
            ("col", short_input),
            ("col", front),
            ("col", short_taps),
            ("col", query_short),
            ("col", key_long),
            ("col", grad),
            ("col", short_back),
            ("col", long_rate),
            ("all", forward_full),
            ("all", forward_two),
            ("all", forward_three),
            ("all", inverse_high),
            ("all", inverse_lags),
        ],
        [
            ("col", col, BF16),
            ("col", col, BF16),
            ("col", col, BF16),
            ("state", state_shape, F32),
            ("col", (N, channels), F32),
            ("col", (T, channels), F32),
        ],
        [pltpu.VMEM((T, width), F32)],
        10**6,
    )
    earlier, taps_grad = exchange_states_and_lags(
        states.reshape(piece_shape), rate_piece, lags, sequence**-0.5
    )
    earlier = earlier.reshape(state_shape)
    core_output, query_long_grad, key_short_grad, value_short_grad = over_blocks(
        rear_kernel,
        width,
        channels,
        [
            ("col", long_input),
            ("col", filter_spec),
            ("state", earlier),
            ("col", long_residue),
            ("col", long_rate),
            ("col", query_long),
            ("col", cotangent),
            ("col", short_back),
            ("col", behind),
            ("col", taps_spec),
            ("col", key_short),
            ("col", value_short),
            ("all", forward_full),
            ("all", forward_two),
            ("all", inverse_low),
        ],
        [("col", col, BF16)] * 4,
        [pltpu.VMEM((T, width), F32)],
        10**6,
    )
    return (
        core_output,
        query_short_grad,
        key_short_grad,
        value_short_grad,
        query_long_grad,
        key_long_grad,
        taps_grad,
    )


def solution(mesh):
    tokens = P("ctx", "ch")
    table = P(None, "ch")
    return jax.shard_map(
        local,
        mesh=mesh,
        in_specs=(tokens, tokens, tokens, table, tokens, tokens, table, table, tokens),
        out_specs=(tokens, tokens, tokens, tokens, tokens, tokens, table),
        check_vma=False,
    )
```

```python
import functools
import types

import jax
import jax.numpy as jnp
import ml_dtypes
import numpy as np
from jax import lax
from jax.experimental import pallas as pl
from jax.experimental.pallas import tpu as pltpu
from jax.sharding import PartitionSpec as P

F32 = jnp.float32
BF16 = jnp.bfloat16
T = 128
N = 2 * T
LANES = 128
VMEM_LIMIT = 40 * 1024 * 1024
CHIPS_X = 4
ROW = 2 * CHIPS_X
WIDTH = 512
MESH = pl.DeviceIdType.MESH


def forward_table():
    n = np.arange(N)
    k = np.arange(T)
    angle = 2.0 * np.pi * ((k[:, None] * n[None, :]) % N) / N
    low = -np.sin(angle)
    low[0] = (-1.0) ** n
    return np.concatenate([np.cos(angle), low], axis=0)


def inverse_table(rows):
    n = np.asarray(rows)
    k = np.arange(T)
    angle = 2.0 * np.pi * ((n[:, None] * k[None, :]) % N) / N
    weight = np.full((T,), 2.0 / N)
    weight[0] = 1.0 / N
    low = -np.sin(angle) * weight
    low[:, 0] = (-1.0) ** n / N
    return np.concatenate([np.cos(angle) * weight, low], axis=1)


def halves(table):
    high = table.astype(ml_dtypes.bfloat16)
    low = (table - high.astype(np.float64)).astype(ml_dtypes.bfloat16)
    return high, low


def two_terms(table):
    high, low = halves(table)
    return np.concatenate([high, low], axis=1)


def three_terms(table):
    high, low = halves(table)
    return np.concatenate([high, low, high], axis=1)


def dot(table, data):
    return jnp.dot(table, data, preferred_element_type=F32)


def exact(data):
    return jnp.concatenate([data, data], axis=0)


def split(data):
    high = data.astype(BF16)
    low = (data - high.astype(F32)).astype(BF16)
    return jnp.concatenate([high, high, low], axis=0)


def product(first, second, conjugate):
    ar, ai = first[:T], first[T:]
    br, bi = second[:T], second[T:]
    top = lax.broadcasted_iota(jnp.int32, ar.shape, 0) == 0
    rr, ii = ar * br, ai * bi
    if conjugate:
        re = rr + jnp.where(top, 0.0, ii)
        im = jnp.where(top, ii, ai * br - ar * bi)
    else:
        re = rr - jnp.where(top, 0.0, ii)
        im = jnp.where(top, ii, ai * br + ar * bi)
    return jnp.concatenate([re, im], axis=0)


def rows_iota():
    return lax.broadcasted_iota(jnp.int32, (8, LANES), 0).astype(F32)


def state_sums(data, rate, newest_last):
    iota = rows_iota()
    powers = (7.0 - iota) if newest_last else iota
    order = range(T // 8) if newest_last else range(T // 8 - 1, -1, -1)
    tiles = [data[8 * q : 8 * q + 8] for q in order]
    rows = []
    for m in range(rate.shape[0]):
        a = rate[m : m + 1]
        step = jnp.broadcast_to(jnp.exp(-8.0 * a), (8, LANES))
        total = tiles[0]
        for tile in tiles[1:]:
            total = total * step + tile
        rows.append(jnp.sum(total * jnp.exp(-a * powers), axis=0, keepdims=True))
    return rows


def mode_series(out_ref, lanes, scales, rate, powers, rising):
    steps, terms = [], []
    for m in range(rate.shape[0]):
        a = rate[m : m + 1]
        steps.append(jnp.broadcast_to(jnp.exp(-8.0 * a), (8, LANES)))
        terms.append(scales[m] * jnp.exp(-a * powers))
    order = range(T // 8) if rising else range(T // 8 - 1, -1, -1)
    for place, q in enumerate(order):
        if place:
            terms = [term * step for term, step in zip(terms, steps)]
        layer = terms
        while len(layer) > 1:
            layer = [layer[i] + layer[i + 1] for i in range(0, len(layer), 2)]
        out_ref[8 * q : 8 * q + 8, lanes] = layer[0]


def send(source, target, peer, send_sem, recv_sem):
    copy = pltpu.make_async_remote_copy(
        src_ref=source,
        dst_ref=target,
        send_sem=send_sem,
        recv_sem=recv_sem,
        device_id={"ctx": peer},
        device_id_type=MESH,
    )
    copy.start()
    return copy


def wait_bytes(ref, sem):
    pltpu.make_async_copy(ref, ref, sem).wait()


def each(low, high, body):
    lax.fori_loop(low, high, lambda i, _: (body(i), 0)[1], 0)


class Place:
    def __init__(self, count):
        self.count = count
        self.me = lax.axis_index("ctx")
        self.core = lax.rem(self.me, 2)
        self.along_x = lax.rem(self.me // 2, CHIPS_X)
        self.in_row = lax.rem(self.me, ROW)
        self.row = self.me // ROW
        self.far = lax.rem(self.row, 2)
        self.along_y = self.row // 2
        self.rows = count // ROW
        self.planes = count // 4
        self.spot = self.along_y * CHIPS_X + self.along_x
        self.sibling = self.me + 1 - 2 * self.core
        self.partner = self.me + ROW * (1 - 2 * self.far)

    def row_peer(self, i):
        return lax.rem(self.in_row + i, ROW)

    def plane_device(self, spot):
        return (spot // CHIPS_X * 2 + self.far) * ROW + lax.rem(spot, CHIPS_X) * 2 + self.core


def greet(here):
    barrier = pltpu.get_barrier_semaphore()

    def signal(device):
        pl.semaphore_signal(barrier, inc=1, device_id={"ctx": device}, device_id_type=MESH)

    each(1, ROW, lambda i: signal(here.row * ROW + here.row_peer(i)))
    each(1, here.rows, lambda i: signal(lax.rem(here.row + i, here.rows) * ROW + here.in_row))
    chips_y = here.rows // 2
    for i in range(1, CHIPS_X):
        for j in range(1, chips_y):
            spot = lax.rem(here.along_y + j, chips_y) * CHIPS_X + lax.rem(
                here.along_x + i, CHIPS_X
            )
            signal(here.plane_device(spot))
    signal(lax.rem(here.me + 1, here.count))
    signal(lax.rem(here.me + here.count - 1, here.count))
    greeted = ROW - 1 + here.rows - 1 + (CHIPS_X - 1) * (chips_y - 1) + 2

    def finish():
        pl.semaphore_wait(barrier, greeted)

    return finish


class Carry:
    def __init__(self, here, refs, name, later, rate_ref):
        self.here, self.later, self.rate_ref = here, later, rate_ref
        for part in ("sums", "row", "local", "total", "rows", "out", "got", "sems", "row_sems"):
            setattr(self, part, getattr(refs, name + "_" + part))
        self.peers = pl.ds(0, ROW - 1)

    def to_row(self, source, target, send_sem, recv_sem):
        here = self.here

        def body(i):
            peer = here.row_peer(i)
            send(
                source.at[peer], target.at[here.in_row], here.row * ROW + peer, send_sem, recv_sem
            )

        each(1, ROW, body)
        target[here.in_row] = source[here.in_row]

    def step(self):
        lanes = self.got.shape[2]
        own = pl.ds(pl.multiple_of(self.here.in_row * lanes, LANES), lanes)
        return self.rate_ref[:, own]

    def order(self):
        return range(ROW - 1, -1, -1) if self.later else range(ROW)

    def first(self):
        self.to_row(self.sums, self.row, self.sems.at[0], self.sems.at[1])

    def column_ranges(self):
        row, rows = self.here.row, self.here.rows
        after, before = (row + 1, rows), (0, row)
        return (before, after) if self.later else (after, before)

    def second(self):
        here = self.here
        wait_bytes(self.row.at[self.peers], self.sems.at[1])
        step = jnp.exp(-float(T) * self.step())
        carry = jnp.zeros(step.shape, F32)
        for k in self.order():
            self.local[k] = carry
            carry = carry * step + self.row[k]
        self.total[...] = carry
        targets, _ = self.column_ranges()
        each(
            *targets,
            lambda k: send(
                self.total,
                self.rows.at[here.row],
                k * ROW + here.in_row,
                self.row_sems.at[0, k],
                self.row_sems.at[1, here.row],
            ),
        )

    def third(self):
        here = self.here
        _, (low, high) = self.column_ranges()
        each(low, high, lambda k: wait_bytes(self.total, self.row_sems.at[1, k]))
        rate = self.step()
        leap = jnp.exp(-float(T * ROW) * rate)

        def body(i, carry):
            k = high - 1 - (i - low) if self.later else i
            return carry * leap + self.rows[k]

        carry = lax.fori_loop(low, high, body, jnp.zeros(rate.shape, F32))
        step = jnp.exp(-float(T) * rate)
        for k in self.order():
            self.out[k] = self.local[k] + carry
            carry = carry * step
        self.to_row(self.out, self.got, self.sems.at[2], self.sems.at[3])

    def arrive(self):
        wait_bytes(self.got.at[self.peers], self.sems.at[3])

    def settle(self):
        targets, _ = self.column_ranges()
        wait_bytes(self.sums.at[self.peers], self.sems.at[0])
        each(*targets, lambda k: wait_bytes(self.total, self.row_sems.at[0, k]))
        wait_bytes(self.out.at[self.peers], self.sems.at[2])


def put_states(out_ref, block, group, rows):
    half = group % 2 * LANES
    for m, row in enumerate(rows):
        out_ref[block * (WIDTH // 256) + group // 2, m : m + 1, half : half + LANES] = row


def take_scales(states_ref, block, group, residue):
    half = group % 2 * LANES
    states = states_ref[block * (WIDTH // 256) + group // 2, :, half : half + LANES]
    scaled = residue * states
    return [scaled[m : m + 1] for m in range(residue.shape[0])]


def core_kernel(*refs, names, loads, count, scale):
    r = types.SimpleNamespace(**dict(zip(names, refs)))
    here = Place(count)
    channels = r.long_rate.shape[1]
    blocks = channels // WIDTH
    groups = WIDTH // LANES

    copies = {
        name: pltpu.make_async_copy(getattr(r, name + "_hbm"), getattr(r, name), r.load_sems.at[k])
        for k, name in enumerate(loads)
    }
    for name in loads:
        copies[name].start()
    met = greet(here)

    def need(*wanted):
        for name in wanted:
            copies[name].wait()

    def cols(block):
        return pl.ds(pl.multiple_of(block * WIDTH, WIDTH), WIDTH)

    def lanes_of(block, group):
        return pl.ds(pl.multiple_of(block * WIDTH + group * LANES, LANES), LANES)

    def wide(ref, block):
        return ref[:, cols(block)].astype(F32)

    need("key_short", "value_short")

    def make_short_input(b):
        r.extended[T:, cols(b)] = (wide(r.key_short, b) * wide(r.value_short, b)).astype(BF16)

    each(0, blocks, make_short_input)
    met()
    last = count - 1
    own_rows, before_rows = pl.ds(T, T), pl.ds(0, T)

    @pl.when(here.me < last)
    def _():
        send(
            r.extended.at[own_rows],
            r.extended.at[before_rows],
            here.me + 1,
            r.halo_sems.at[0],
            r.halo_sems.at[1],
        )

    @pl.when(here.me == 0)
    def _():
        r.extended[:T] = jnp.zeros((T, channels), BF16)

    need("long_rate", "query_long", "cotangent")

    def make_back_states(b):
        for group in range(groups):
            lanes = lanes_of(b, group)
            back = r.query_long[:, lanes].astype(F32) * r.cotangent[:, lanes].astype(F32)
            put_states(r.later_sums, b, group, state_sums(back, r.long_rate[:, lanes], False))

    each(0, blocks, make_back_states)
    later = Carry(here, r, "later", True, r.long_rate)
    later.first()

    need("long_residue", "forward_three")
    iota = rows_iota()

    def make_filter(b):
        for group in range(groups):
            lanes = lanes_of(b, group)
            rate, residue = r.long_rate[:, lanes], r.long_residue[:, lanes]
            scales = [residue[m : m + 1] for m in range(rate.shape[0])]
            mode_series(
                r.block_scr, pl.ds(group * LANES, LANES), scales, rate, iota, True
            )
        r.filter_spec[:, cols(b)] = dot(r.forward_three[...], split(r.block_scr[...]))

    each(0, blocks, make_filter)
    later.second()

    need("inverse_low", "short_taps")

    def make_local_grad(b):
        back = wide(r.query_long, b) * wide(r.cotangent, b)
        spectrum = dot(r.forward_three[...], split(back))
        turned = product(spectrum, r.filter_spec[:, cols(b)], True)
        r.long_part[:, cols(b)] = dot(r.inverse_low[...], split(turned))
        r.taps_spec[:, cols(b)] = dot(r.forward_three[...], split(r.short_taps[:, cols(b)]))

    each(0, blocks, make_local_grad)
    later.third()
    need("key_long", "query_short", "forward_two")
    later.arrive()

    def make_long_grad(b):
        for group in range(groups):
            lanes = lanes_of(b, group)
            rate, residue = r.long_rate[:, lanes], r.long_residue[:, lanes]
            scales = take_scales(r.later_got, b, group, residue)
            mode_series(
                r.block_scr, pl.ds(group * LANES, LANES), scales, rate, 8.0 - iota, False
            )
        grad = (r.long_part[:, cols(b)] + r.block_scr[...]).astype(BF16)
        r.long_grad[:, cols(b)] = grad
        hidden_grad = grad.astype(F32) * wide(r.key_long, b)
        r.back_ext[:T, cols(b)] = (hidden_grad * wide(r.query_short, b)).astype(BF16)

    each(0, blocks, make_long_grad)

    @pl.when(here.me > 0)
    def _():
        send(
            r.back_ext.at[before_rows],
            r.back_ext.at[own_rows],
            here.me - 1,
            r.halo_sems.at[2],
            r.halo_sems.at[3],
        )

    @pl.when(here.me == last)
    def _():
        r.back_ext[T:] = jnp.zeros((T, channels), BF16)

    need("forward_full", "inverse_high", "inverse_lags")

    def own_spectrum(b):
        r.own_spec[:, cols(b)] = dot(r.forward_two[...], exact(r.back_ext[:T, cols(b)]))

    each(0, blocks, own_spectrum)

    @pl.when(here.me > 0)
    def _():
        wait_bytes(r.extended.at[before_rows], r.halo_sems.at[1])

    def make_hidden(b):
        spectrum = dot(r.forward_full[...], exact(r.extended[:, cols(b)]))
        r.input_spec[:, cols(b)] = spectrum
        turned = product(spectrum, r.taps_spec[:, cols(b)], False)
        short_mix = dot(r.inverse_high[...], split(turned))
        hidden = (wide(r.query_short, b) * short_mix).astype(BF16).astype(F32)
        key, grad = wide(r.key_long, b), wide(r.long_grad, b)
        r.key_long_grad[:, cols(b)] = (grad * hidden).astype(BF16)
        r.query_short_grad[:, cols(b)] = (grad * key * short_mix).astype(BF16)
        long_input = (key * hidden).astype(BF16)
        r.long_input[:, cols(b)] = long_input
        r.block_scr[...] = long_input.astype(F32)
        for group in range(groups):
            rows = state_sums(
                r.block_scr[:, group * LANES : (group + 1) * LANES],
                r.long_rate[:, lanes_of(b, group)],
                True,
            )
            put_states(r.earlier_sums, b, group, rows)

    each(0, blocks, make_hidden)
    earlier = Carry(here, r, "earlier", False, r.long_rate)
    earlier.first()

    half = channels // 2
    mine = pl.ds(pl.multiple_of(here.core * half, LANES), half)
    theirs = pl.ds(pl.multiple_of((1 - here.core) * half, LANES), half)

    def make_lags(b):
        turned = product(r.input_spec[:, cols(b)], r.own_spec[:, cols(b)], True)
        r.lags[:, cols(b)] = dot(r.inverse_lags[...], split(turned))

    each(0, blocks, make_lags)
    to_sibling = send(
        r.lags.at[:, theirs], r.half_scr, here.sibling, r.lag_sems.at[0, 0], r.lag_sems.at[1, 0]
    )
    earlier.second()

    to_sibling.wait()
    r.sum_scr[...] = (r.lags[:, mine] + r.half_scr[...]).reshape(r.sum_scr.shape)

    def to_plane(i):
        spot = lax.rem(here.spot + i, here.planes)
        send(
            r.sum_scr.at[spot],
            r.plane_scr.at[here.spot],
            here.plane_device(spot),
            r.lag_sems.at[0, 1],
            r.lag_sems.at[1, 1],
        )

    each(1, here.planes, to_plane)
    r.plane_scr[here.spot] = r.sum_scr[here.spot]

    def make_local_mix(b):
        spectrum = dot(r.forward_two[...], exact(r.long_input[:, cols(b)]))
        turned = product(spectrum, r.filter_spec[:, cols(b)], False)
        r.long_part[:, cols(b)] = dot(r.inverse_low[...], split(turned))

    each(0, blocks, make_local_mix)
    earlier.third()

    plane_rest = pl.ds(0, here.planes - 1)
    wait_bytes(r.plane_scr.at[plane_rest], r.lag_sems.at[1, 1])
    total = r.plane_scr[0]
    for spot in range(1, here.planes):
        total = total + r.plane_scr[spot]
    r.own_scr[...] = total
    to_partner = send(
        r.own_scr, r.pair_scr, here.partner, r.lag_sems.at[0, 2], r.lag_sems.at[1, 2]
    )
    earlier.arrive()

    def make_core(b):
        for group in range(groups):
            lanes = lanes_of(b, group)
            rate, residue = r.long_rate[:, lanes], r.long_residue[:, lanes]
            scales = take_scales(r.earlier_got, b, group, residue)
            mode_series(
                r.block_scr, pl.ds(group * LANES, LANES), scales, rate, iota + 1.0, True
            )
        long_mix = r.long_part[:, cols(b)] + r.block_scr[...]
        r.core_output[:, cols(b)] = (wide(r.query_long, b) * long_mix).astype(BF16)
        r.query_long_grad[:, cols(b)] = (wide(r.cotangent, b) * long_mix).astype(BF16)

    each(0, blocks, make_core)

    to_partner.wait()
    r.own_scr[...] = (r.own_scr[...] + r.pair_scr[...]) * scale
    mine_rows = pl.ds(pl.multiple_of(here.spot * 8, 8), 8)

    def from_plane(i):
        spot = lax.rem(here.spot + i, here.planes)
        send(
            r.own_scr,
            r.taps_grad.at[mine_rows, mine],
            here.plane_device(spot),
            r.lag_sems.at[0, 3],
            r.lag_sems.at[1, 3],
        )

    each(1, here.planes, from_plane)
    r.taps_grad[mine_rows, mine] = r.own_scr[...]

    @pl.when(here.me < last)
    def _():
        wait_bytes(r.back_ext.at[own_rows], r.halo_sems.at[3])

    def make_short_grads(b):
        back = dot(r.forward_full[...], exact(r.back_ext[:, cols(b)]))
        turned = product(back, r.taps_spec[:, cols(b)], True)
        input_grad = dot(r.inverse_low[...], split(turned))
        r.key_short_grad[:, cols(b)] = (input_grad * wide(r.value_short, b)).astype(BF16)
        r.value_short_grad[:, cols(b)] = (input_grad * wide(r.key_short, b)).astype(BF16)

    each(0, blocks, make_short_grads)

    wait_bytes(r.plane_scr.at[plane_rest], r.lag_sems.at[1, 3])
    send(
        r.taps_grad.at[:, mine],
        r.taps_grad.at[:, mine],
        here.sibling,
        r.lag_sems.at[0, 4],
        r.lag_sems.at[1, 4],
    ).wait()

    later.settle()
    earlier.settle()
    wait_bytes(r.sum_scr.at[plane_rest], r.lag_sems.at[0, 1])
    wait_bytes(r.sum_scr.at[plane_rest], r.lag_sems.at[0, 3])

    @pl.when(here.me < last)
    def _():
        wait_bytes(r.extended.at[own_rows], r.halo_sems.at[0])

    @pl.when(here.me > 0)
    def _():
        wait_bytes(r.back_ext.at[before_rows], r.halo_sems.at[2])


def local(
    query_short,
    key_short,
    value_short,
    short_taps,
    query_long,
    key_long,
    long_residue,
    long_rate,
    cotangent,
):
    count = lax.axis_size("ctx")
    tokens_here, channels = query_short.shape
    modes = long_rate.shape[0]
    sequence = tokens_here * count
    planes = count // 4
    rows = count // ROW
    own_lanes = channels // ROW

    forward = forward_table()
    inputs = {
        "key_short": key_short,
        "value_short": value_short,
        "long_rate": long_rate,
        "query_long": query_long,
        "cotangent": cotangent,
        "long_residue": long_residue,
        "forward_three": jnp.asarray(three_terms(forward[:, :T])),
        "inverse_low": jnp.asarray(three_terms(inverse_table(np.arange(T)))),
        "short_taps": short_taps,
        "key_long": key_long,
        "query_short": query_short,
        "forward_two": jnp.asarray(two_terms(forward[:, :T])),
        "forward_full": jnp.asarray(two_terms(forward)),
        "inverse_high": jnp.asarray(three_terms(inverse_table(np.arange(T) + T))),
        "inverse_lags": jnp.asarray(three_terms(inverse_table(T - np.arange(T)))),
    }
    tokens = (tokens_here, channels)
    outputs = {
        "core_output": (tokens, BF16),
        "query_short_grad": (tokens, BF16),
        "key_short_grad": (tokens, BF16),
        "value_short_grad": (tokens, BF16),
        "query_long_grad": (tokens, BF16),
        "key_long_grad": (tokens, BF16),
        "taps_grad": (short_taps.shape, F32),
    }
    scratch = {name: pltpu.VMEM(array.shape, array.dtype) for name, array in inputs.items()}
    scratch["load_sems"] = pltpu.SemaphoreType.DMA((len(inputs),))
    state = (modes, own_lanes)
    for name in ("later", "earlier"):
        for part in ("sums", "row", "local", "out", "got"):
            scratch[name + "_" + part] = pltpu.VMEM((ROW,) + state, F32)
        scratch[name + "_total"] = pltpu.VMEM(state, F32)
        scratch[name + "_rows"] = pltpu.VMEM((rows,) + state, F32)
        scratch[name + "_sems"] = pltpu.SemaphoreType.DMA((4,))
        scratch[name + "_row_sems"] = pltpu.SemaphoreType.DMA((2, rows))
    scratch["extended"] = pltpu.VMEM((2 * T, channels), BF16)
    scratch["back_ext"] = pltpu.VMEM((2 * T, channels), BF16)
    scratch["long_grad"] = pltpu.VMEM(tokens, BF16)
    scratch["long_input"] = pltpu.VMEM(tokens, BF16)
    scratch["long_part"] = pltpu.VMEM(tokens, F32)
    scratch["block_scr"] = pltpu.VMEM((T, WIDTH), F32)
    for name in ("filter_spec", "taps_spec", "input_spec", "own_spec"):
        scratch[name] = pltpu.VMEM((N, channels), F32)
    scratch["lags"] = pltpu.VMEM((T, channels), F32)
    scratch["half_scr"] = pltpu.VMEM((T, channels // 2), F32)
    scratch["sum_scr"] = pltpu.VMEM((planes, T // planes, channels // 2), F32)
    scratch["plane_scr"] = pltpu.VMEM((planes, T // planes, channels // 2), F32)
    scratch["own_scr"] = pltpu.VMEM((T // planes, channels // 2), F32)
    scratch["pair_scr"] = pltpu.VMEM((T // planes, channels // 2), F32)
    scratch["halo_sems"] = pltpu.SemaphoreType.DMA((4,))
    scratch["lag_sems"] = pltpu.SemaphoreType.DMA((2, 5))

    names = [name + "_hbm" for name in inputs] + list(outputs) + list(scratch)
    return pl.pallas_call(
        functools.partial(
            core_kernel,
            names=tuple(names),
            loads=tuple(inputs),
            count=count,
            scale=sequence**-0.5,
        ),
        in_specs=[pl.BlockSpec(memory_space=pl.ANY)] * len(inputs),
        out_specs=[pl.BlockSpec(memory_space=pltpu.VMEM)] * len(outputs),
        out_shape=[jax.ShapeDtypeStruct(shape, dtype) for shape, dtype in outputs.values()],
        scratch_shapes=list(scratch.values()),
        compiler_params=pltpu.CompilerParams(
            collective_id=0, has_side_effects=True, vmem_limit_bytes=VMEM_LIMIT
        ),
    )(*inputs.values())


def solution(mesh):
    tokens = P("ctx", "ch")
    table = P(None, "ch")
    return jax.shard_map(
        local,
        mesh=mesh,
        in_specs=(tokens, tokens, tokens, table, tokens, tokens, table, table, tokens),
        out_specs=(tokens, tokens, tokens, tokens, tokens, tokens, table),
        check_vma=False,
    )
```

```python
import functools
import types

import jax
import jax.numpy as jnp
import ml_dtypes
import numpy as np
from jax import lax
from jax.experimental import pallas as pl
from jax.experimental.pallas import tpu as pltpu
from jax.sharding import PartitionSpec as P

F32 = jnp.float32
BF16 = jnp.bfloat16
T = 128
N = 2 * T
LANES = 128
VMEM_LIMIT = 63 * 1024 * 1024
CHIPS_X = 4
ROW = 2 * CHIPS_X
WIDTH = 512
MESH = pl.DeviceIdType.MESH


def forward_table():
    n = np.arange(N)
    k = np.arange(T)
    angle = 2.0 * np.pi * ((k[:, None] * n[None, :]) % N) / N
    low = -np.sin(angle)
    low[0] = (-1.0) ** n
    return np.concatenate([np.cos(angle), low], axis=0)


def inverse_table(rows):
    n = np.asarray(rows)
    k = np.arange(T)
    angle = 2.0 * np.pi * ((n[:, None] * k[None, :]) % N) / N
    weight = np.full((T,), 2.0 / N)
    weight[0] = 1.0 / N
    low = -np.sin(angle) * weight
    low[:, 0] = (-1.0) ** n / N
    return np.concatenate([np.cos(angle) * weight, low], axis=1)


def halves(table):
    high = table.astype(ml_dtypes.bfloat16)
    low = (table - high.astype(np.float64)).astype(ml_dtypes.bfloat16)
    return high, low


def two_terms(table):
    high, low = halves(table)
    return np.concatenate([high, low], axis=1)


def three_terms(table):
    high, low = halves(table)
    return np.concatenate([high, low, high], axis=1)


def dot(table, data):
    return jnp.dot(table, data, preferred_element_type=F32)


def exact(data):
    return jnp.concatenate([data, data], axis=0)


def split(data):
    high = data.astype(BF16)
    low = (data - high.astype(F32)).astype(BF16)
    return jnp.concatenate([high, high, low], axis=0)


def product(first, second, conjugate):
    ar, ai = first[:T], first[T:]
    br, bi = second[:T], second[T:]
    top = lax.broadcasted_iota(jnp.int32, ar.shape, 0) == 0
    rr, ii = ar * br, ai * bi
    if conjugate:
        re = rr + jnp.where(top, 0.0, ii)
        im = jnp.where(top, ii, ai * br - ar * bi)
    else:
        re = rr - jnp.where(top, 0.0, ii)
        im = jnp.where(top, ii, ai * br + ar * bi)
    return jnp.concatenate([re, im], axis=0)


def rows_iota():
    return lax.broadcasted_iota(jnp.int32, (8, LANES), 0).astype(F32)


def state_sums(data, rate, newest_last):
    iota = rows_iota()
    powers = (7.0 - iota) if newest_last else iota
    order = range(T // 8) if newest_last else range(T // 8 - 1, -1, -1)
    tiles = [data[8 * q : 8 * q + 8] for q in order]
    rows = []
    steps = jnp.exp(-8.0 * rate)
    for m in range(rate.shape[0]):
        a = rate[m : m + 1]
        step = jnp.broadcast_to(steps[m : m + 1], (8, LANES))
        total = tiles[0]
        for tile in tiles[1:]:
            total = total * step + tile
        rows.append(jnp.sum(total * jnp.exp(-a * powers), axis=0, keepdims=True))
    return rows


def mode_series(out_ref, lanes, scales, rate, powers, rising):
    steps, terms = [], []
    decay = jnp.exp(-8.0 * rate)
    for m in range(rate.shape[0]):
        a = rate[m : m + 1]
        steps.append(jnp.broadcast_to(decay[m : m + 1], (8, LANES)))
        terms.append(scales[m] * jnp.exp(-a * powers))
    order = range(T // 8) if rising else range(T // 8 - 1, -1, -1)
    for place, q in enumerate(order):
        if place:
            terms = [term * step for term, step in zip(terms, steps)]
        layer = terms
        while len(layer) > 1:
            layer = [layer[i] + layer[i + 1] for i in range(0, len(layer), 2)]
        out_ref[8 * q : 8 * q + 8, lanes] = layer[0]


def send(source, target, peer, send_sem, recv_sem):
    copy = pltpu.make_async_remote_copy(
        src_ref=source,
        dst_ref=target,
        send_sem=send_sem,
        recv_sem=recv_sem,
        device_id={"ctx": peer},
        device_id_type=MESH,
    )
    copy.start()
    return copy


def wait_bytes(ref, sem):
    pltpu.make_async_copy(ref, ref, sem).wait()


def each(low, high, body):
    lax.fori_loop(low, high, lambda i, _: (body(i), 0)[1], 0)


class Place:
    def __init__(self, count):
        self.count = count
        self.me = lax.axis_index("ctx")
        self.core = lax.rem(self.me, 2)
        self.along_x = lax.rem(self.me // 2, CHIPS_X)
        self.in_row = lax.rem(self.me, ROW)
        self.row = self.me // ROW
        self.far = lax.rem(self.row, 2)
        self.along_y = self.row // 2
        self.rows = count // ROW
        self.planes = count // 4
        self.spot = self.along_y * CHIPS_X + self.along_x
        self.sibling = self.me + 1 - 2 * self.core
        self.partner = self.me + ROW * (1 - 2 * self.far)

    def row_peer(self, i):
        return lax.rem(self.in_row + i, ROW)

    def plane_device(self, spot):
        return (spot // CHIPS_X * 2 + self.far) * ROW + lax.rem(spot, CHIPS_X) * 2 + self.core


def greet(here):
    barrier = pltpu.get_barrier_semaphore()

    def signal(device):
        pl.semaphore_signal(barrier, inc=1, device_id={"ctx": device}, device_id_type=MESH)

    each(1, ROW, lambda i: signal(here.row * ROW + here.row_peer(i)))
    each(1, here.rows, lambda i: signal(lax.rem(here.row + i, here.rows) * ROW + here.in_row))
    chips_y = here.rows // 2
    for i in range(1, CHIPS_X):
        for j in range(1, chips_y):
            spot = lax.rem(here.along_y + j, chips_y) * CHIPS_X + lax.rem(
                here.along_x + i, CHIPS_X
            )
            signal(here.plane_device(spot))
    signal(lax.rem(here.me + 1, here.count))
    signal(lax.rem(here.me + here.count - 1, here.count))
    greeted = ROW - 1 + here.rows - 1 + (CHIPS_X - 1) * (chips_y - 1) + 2

    def finish():
        pl.semaphore_wait(barrier, greeted)

    return finish


class Carry:
    def __init__(self, here, refs, name, later, rate_ref):
        self.here, self.later, self.rate_ref = here, later, rate_ref
        for part in ("sums", "row", "local", "total", "rows", "out", "got", "sems", "row_sems"):
            setattr(self, part, getattr(refs, name + "_" + part))
        self.peers = pl.ds(0, ROW - 1)

    def to_row(self, source, target, send_sem, recv_sem):
        here = self.here

        def body(i):
            peer = here.row_peer(i)
            send(
                source.at[peer], target.at[here.in_row], here.row * ROW + peer, send_sem, recv_sem
            )

        each(1, ROW, body)
        target[here.in_row] = source[here.in_row]

    def step(self):
        lanes = self.got.shape[2]
        own = pl.ds(pl.multiple_of(self.here.in_row * lanes, LANES), lanes)
        return self.rate_ref[:, own]

    def order(self):
        return range(ROW - 1, -1, -1) if self.later else range(ROW)

    def first(self):
        self.to_row(self.sums, self.row, self.sems.at[0], self.sems.at[1])

    def column_ranges(self):
        row, rows = self.here.row, self.here.rows
        after, before = (row + 1, rows), (0, row)
        return (before, after) if self.later else (after, before)

    def second(self):
        here = self.here
        wait_bytes(self.row.at[self.peers], self.sems.at[1])
        step = jnp.exp(-float(T) * self.step())
        carry = jnp.zeros(step.shape, F32)
        for k in self.order():
            self.local[k] = carry
            carry = carry * step + self.row[k]
        self.total[...] = carry
        targets, _ = self.column_ranges()
        each(
            *targets,
            lambda k: send(
                self.total,
                self.rows.at[here.row],
                k * ROW + here.in_row,
                self.row_sems.at[0, k],
                self.row_sems.at[1, here.row],
            ),
        )

    def third(self):
        here = self.here
        _, (low, high) = self.column_ranges()
        each(low, high, lambda k: wait_bytes(self.total, self.row_sems.at[1, k]))
        rate = self.step()
        leap = jnp.exp(-float(T * ROW) * rate)

        def body(i, carry):
            k = high - 1 - (i - low) if self.later else i
            return carry * leap + self.rows[k]

        carry = lax.fori_loop(low, high, body, jnp.zeros(rate.shape, F32))
        step = jnp.exp(-float(T) * rate)
        for k in self.order():
            self.out[k] = self.local[k] + carry
            carry = carry * step
        self.to_row(self.out, self.got, self.sems.at[2], self.sems.at[3])

    def arrive(self):
        wait_bytes(self.got.at[self.peers], self.sems.at[3])

    def settle(self):
        targets, _ = self.column_ranges()
        wait_bytes(self.sums.at[self.peers], self.sems.at[0])
        each(*targets, lambda k: wait_bytes(self.total, self.row_sems.at[0, k]))
        wait_bytes(self.out.at[self.peers], self.sems.at[2])


class Halo:
    def __init__(self, here, buffer, source_rows, target_rows, onward, relays, sems):
        self.here, self.sems = here, sems
        self.source, self.target = buffer.at[source_rows], buffer.at[target_rows]
        self.held, self.passed = relays
        self.step = 1 if onward else -1
        first, last = here.in_row == 0, here.in_row == ROW - 1
        low, high = here.row > 0, here.row < here.rows - 1
        self.leaves, self.enters = (last, first) if onward else (first, last)
        self.sends_row, self.takes_row = (high, low) if onward else (low, high)
        self.entry = 0 if onward else ROW - 1
        self.piece = buffer.shape[1] // ROW

    def lanes(self, j):
        return pl.ds(pl.multiple_of(j * self.piece, self.piece), self.piece)

    def first(self):
        here, sems = self.here, self.sems

        @pl.when(jnp.logical_not(self.leaves))
        def _():
            send(self.source, self.target, here.me + self.step, sems.at[0], sems.at[1])

        @pl.when(self.leaves & self.sends_row)
        def _():
            def body(i):
                j = here.row_peer(i)
                send(
                    self.source.at[:, self.lanes(j)],
                    self.held,
                    here.row * ROW + j,
                    sems.at[2],
                    sems.at[3],
                )

            each(1, ROW, body)

    def second(self):
        here, sems = self.here, self.sems
        over = here.me + self.step * ROW
        own = self.lanes(here.in_row)

        @pl.when(self.sends_row & self.leaves)
        def _():
            send(self.source.at[:, own], self.passed, over, sems.at[4], sems.at[5])

        @pl.when(self.sends_row & jnp.logical_not(self.leaves))
        def _():
            wait_bytes(self.held, sems.at[3])

        @pl.when(self.sends_row & self.enters)
        def _():
            send(self.held, self.target.at[:, own], over, sems.at[4], sems.at[1])

        @pl.when(self.sends_row & jnp.logical_not(self.enters | self.leaves))
        def _():
            send(self.held, self.passed, over, sems.at[4], sems.at[5])

    def third(self):
        here, sems = self.here, self.sems

        @pl.when(self.takes_row & jnp.logical_not(self.enters))
        def _():
            wait_bytes(self.passed, sems.at[5])
            send(
                self.passed,
                self.target.at[:, self.lanes(here.in_row)],
                here.row * ROW + self.entry,
                sems.at[6],
                sems.at[1],
            )

    def arrive(self):
        @pl.when(self.takes_row | jnp.logical_not(self.enters))
        def _():
            wait_bytes(self.target, self.sems.at[1])

    def settle(self):
        sems = self.sems

        @pl.when(jnp.logical_not(self.leaves))
        def _():
            wait_bytes(self.source, sems.at[0])

        @pl.when(self.leaves & self.sends_row)
        def _():
            wait_bytes(self.source.at[:, pl.ds(0, (ROW - 1) * self.piece)], sems.at[2])

        @pl.when(self.sends_row)
        def _():
            wait_bytes(self.held, sems.at[4])

        @pl.when(self.takes_row & jnp.logical_not(self.enters))
        def _():
            wait_bytes(self.passed, sems.at[6])


def put_states(out_ref, block, group, rows):
    half = group % 2 * LANES
    for m, row in enumerate(rows):
        out_ref[block * (WIDTH // 256) + group // 2, m : m + 1, half : half + LANES] = row


def take_scales(states_ref, block, group, residue):
    half = group % 2 * LANES
    states = states_ref[block * (WIDTH // 256) + group // 2, :, half : half + LANES]
    scaled = residue * states
    return [scaled[m : m + 1] for m in range(residue.shape[0])]


def core_kernel(*refs, names, loads, count, scale):
    r = types.SimpleNamespace(**dict(zip(names, refs)))
    here = Place(count)
    channels = r.long_rate.shape[1]
    blocks = channels // WIDTH
    groups = WIDTH // LANES

    copies = {
        name: pltpu.make_async_copy(getattr(r, name + "_hbm"), getattr(r, name), r.load_sems.at[k])
        for k, name in enumerate(loads)
    }
    for name in loads:
        copies[name].start()
    met = greet(here)

    def need(*wanted):
        for name in wanted:
            copies[name].wait()

    def cols(block):
        return pl.ds(pl.multiple_of(block * WIDTH, WIDTH), WIDTH)

    def lanes_of(block, group):
        return pl.ds(pl.multiple_of(block * WIDTH + group * LANES, LANES), LANES)

    def wide(ref, block):
        return ref[:, cols(block)].astype(F32)

    need("key_short", "value_short")

    def make_short_input(b):
        r.extended[T:, cols(b)] = (wide(r.key_short, b) * wide(r.value_short, b)).astype(BF16)

    each(0, blocks, make_short_input)
    last = count - 1
    own_rows, before_rows = pl.ds(T, T), pl.ds(0, T)
    front = Halo(
        here, r.extended, own_rows, before_rows, True, (r.front_held, r.front_passed), r.front_sems
    )
    behind = Halo(
        here,
        r.back_ext,
        before_rows,
        own_rows,
        False,
        (r.behind_held, r.behind_passed),
        r.behind_sems,
    )

    @pl.when(here.me == 0)
    def _():
        r.extended[:T] = jnp.zeros((T, channels), BF16)

    @pl.when(here.me == last)
    def _():
        r.back_ext[T:] = jnp.zeros((T, channels), BF16)

    need("long_rate", "query_long", "cotangent")

    def make_back_states(b):
        for group in range(groups):
            lanes = lanes_of(b, group)
            back = r.query_long[:, lanes].astype(F32) * r.cotangent[:, lanes].astype(F32)
            put_states(r.later_sums, b, group, state_sums(back, r.long_rate[:, lanes], False))

    each(0, blocks, make_back_states)
    later = Carry(here, r, "later", True, r.long_rate)
    met()
    later.first()
    front.first()

    need("long_residue", "forward_three")
    iota = rows_iota()

    def make_filter(b):
        for group in range(groups):
            lanes = lanes_of(b, group)
            rate, residue = r.long_rate[:, lanes], r.long_residue[:, lanes]
            scales = [residue[m : m + 1] for m in range(rate.shape[0])]
            mode_series(
                r.block_scr, pl.ds(group * LANES, LANES), scales, rate, iota, True
            )
        r.filter_spec[:, cols(b)] = dot(r.forward_three[...], split(r.block_scr[...]))

    each(0, blocks, make_filter)
    later.second()
    front.second()

    need("inverse_low", "short_taps")

    def make_local_grad(b):
        back = wide(r.query_long, b) * wide(r.cotangent, b)
        spectrum = dot(r.forward_three[...], split(back))
        turned = product(spectrum, r.filter_spec[:, cols(b)], True)
        r.long_part[:, cols(b)] = dot(r.inverse_low[...], split(turned))
        r.taps_spec[:, cols(b)] = dot(r.forward_three[...], split(r.short_taps[:, cols(b)]))

    each(0, blocks, make_local_grad)
    later.third()
    front.third()
    need("key_long", "query_short", "forward_two")
    later.arrive()

    def make_long_grad(b):
        for group in range(groups):
            lanes = lanes_of(b, group)
            rate, residue = r.long_rate[:, lanes], r.long_residue[:, lanes]
            scales = take_scales(r.later_got, b, group, residue)
            mode_series(
                r.block_scr, pl.ds(group * LANES, LANES), scales, rate, 8.0 - iota, False
            )
        grad = (r.long_part[:, cols(b)] + r.block_scr[...]).astype(BF16)
        r.long_grad[:, cols(b)] = grad
        hidden_grad = grad.astype(F32) * wide(r.key_long, b)
        r.back_ext[:T, cols(b)] = (hidden_grad * wide(r.query_short, b)).astype(BF16)

    each(0, blocks, make_long_grad)
    behind.first()

    need("forward_full", "inverse_high", "inverse_lags")

    def own_spectrum(b):
        r.own_spec[:, cols(b)] = dot(r.forward_two[...], exact(r.back_ext[:T, cols(b)]))

    each(0, blocks, own_spectrum)
    front.arrive()
    half = channels // 2
    mine = pl.ds(pl.multiple_of(here.core * half, LANES), half)
    theirs = pl.ds(pl.multiple_of((1 - here.core) * half, LANES), half)

    def make_lags(b):
        spectrum = dot(r.forward_full[...], exact(r.extended[:, cols(b)]))
        r.input_spec[:, cols(b)] = spectrum
        turned = product(spectrum, r.own_spec[:, cols(b)], True)
        r.lags[:, cols(b)] = dot(r.inverse_lags[...], split(turned))

    each(0, blocks, make_lags)
    to_sibling = send(
        r.lags.at[:, theirs], r.half_scr, here.sibling, r.lag_sems.at[0, 0], r.lag_sems.at[1, 0]
    )
    behind.second()

    def make_hidden(b):
        turned = product(r.input_spec[:, cols(b)], r.taps_spec[:, cols(b)], False)
        short_mix = dot(r.inverse_high[...], split(turned))
        hidden = (wide(r.query_short, b) * short_mix).astype(BF16).astype(F32)
        key, grad = wide(r.key_long, b), wide(r.long_grad, b)
        r.key_long_grad[:, cols(b)] = (grad * hidden).astype(BF16)
        r.query_short_grad[:, cols(b)] = (grad * key * short_mix).astype(BF16)
        long_input = (key * hidden).astype(BF16)
        r.long_input[:, cols(b)] = long_input
        r.block_scr[...] = long_input.astype(F32)
        for group in range(groups):
            rows = state_sums(
                r.block_scr[:, group * LANES : (group + 1) * LANES],
                r.long_rate[:, lanes_of(b, group)],
                True,
            )
            put_states(r.earlier_sums, b, group, rows)

    to_sibling.wait()
    summed = r.lags[:, mine] + r.half_scr[...]
    tile_rows, tile_lanes = r.own_scr.shape
    for spot in range(here.planes):
        top, left = spot // 2 * tile_rows, spot % 2 * tile_lanes
        r.sum_scr[spot] = summed[top : top + tile_rows, left : left + tile_lanes].astype(BF16)

    def to_plane(i):
        spot = lax.rem(here.spot + i, here.planes)
        send(
            r.sum_scr.at[spot],
            r.plane_scr.at[here.spot],
            here.plane_device(spot),
            r.lag_sems.at[0, 1],
            r.lag_sems.at[1, 1],
        )

    each(1, here.planes, to_plane)
    r.plane_scr[here.spot] = r.sum_scr[here.spot]

    each(0, blocks, make_hidden)
    earlier = Carry(here, r, "earlier", False, r.long_rate)
    earlier.first()
    behind.third()

    plane_rest = pl.ds(0, here.planes - 1)
    wait_bytes(r.plane_scr.at[plane_rest], r.lag_sems.at[1, 1])
    total = r.plane_scr[0].astype(F32)
    for spot in range(1, here.planes):
        total = total + r.plane_scr[spot].astype(F32)
    r.own_scr[...] = total
    to_partner = send(
        r.own_scr, r.pair_scr, here.partner, r.lag_sems.at[0, 2], r.lag_sems.at[1, 2]
    )
    earlier.second()

    def make_local_mix(b):
        spectrum = dot(r.forward_two[...], exact(r.long_input[:, cols(b)]))
        turned = product(spectrum, r.filter_spec[:, cols(b)], False)
        r.long_part[:, cols(b)] = dot(r.inverse_low[...], split(turned))

    each(0, blocks, make_local_mix)
    earlier.third()

    to_partner.wait()
    my_rows = pl.ds(pl.multiple_of(here.spot // 2 * tile_rows, tile_rows), tile_rows)
    my_lanes = pl.ds(
        pl.multiple_of(here.core * half + lax.rem(here.spot, 2) * tile_lanes, tile_lanes),
        tile_lanes,
    )
    r.taps_grad[my_rows, my_lanes] = ((r.own_scr[...] + r.pair_scr[...]) * scale).astype(BF16)

    def from_plane(i):
        spot = lax.rem(here.spot + i, here.planes)
        send(
            r.taps_grad.at[my_rows, my_lanes],
            r.taps_grad.at[my_rows, my_lanes],
            here.plane_device(spot),
            r.lag_sems.at[0, 3],
            r.lag_sems.at[1, 3],
        )

    each(1, here.planes, from_plane)
    earlier.arrive()

    def make_core(b):
        for group in range(groups):
            lanes = lanes_of(b, group)
            rate, residue = r.long_rate[:, lanes], r.long_residue[:, lanes]
            scales = take_scales(r.earlier_got, b, group, residue)
            mode_series(
                r.block_scr, pl.ds(group * LANES, LANES), scales, rate, iota + 1.0, True
            )
        long_mix = r.long_part[:, cols(b)] + r.block_scr[...]
        r.core_output[:, cols(b)] = (wide(r.query_long, b) * long_mix).astype(BF16)
        r.query_long_grad[:, cols(b)] = (wide(r.cotangent, b) * long_mix).astype(BF16)

    each(0, blocks, make_core)

    behind.arrive()

    def make_short_grads(b):
        back = dot(r.forward_full[...], exact(r.back_ext[:, cols(b)]))
        turned = product(back, r.taps_spec[:, cols(b)], True)
        input_grad = dot(r.inverse_low[...], split(turned))
        r.key_short_grad[:, cols(b)] = (input_grad * wide(r.value_short, b)).astype(BF16)
        r.value_short_grad[:, cols(b)] = (input_grad * wide(r.key_short, b)).astype(BF16)

    each(0, blocks, make_short_grads)

    wait_bytes(r.plane_scr.at[plane_rest], r.lag_sems.at[1, 3])
    send(
        r.taps_grad.at[:, mine],
        r.taps_grad.at[:, mine],
        here.sibling,
        r.lag_sems.at[0, 4],
        r.lag_sems.at[1, 4],
    ).wait()

    later.settle()
    earlier.settle()
    wait_bytes(r.sum_scr.at[plane_rest], r.lag_sems.at[0, 1])
    wait_bytes(r.sum_scr.at[plane_rest], r.lag_sems.at[0, 3])

    front.settle()
    behind.settle()


def store_kernel(*refs):
    half = len(refs) // 2
    for source, target in zip(refs[:half], refs[half:]):
        target[...] = source[...].astype(target.dtype)


def stored(arrays, types):
    rows, channels = arrays[0].shape
    block = pl.BlockSpec((rows, WIDTH), lambda i: (0, i))
    return pl.pallas_call(
        store_kernel,
        grid=(channels // WIDTH,),
        in_specs=[block] * len(arrays),
        out_specs=[block] * len(arrays),
        out_shape=[jax.ShapeDtypeStruct(a.shape, t) for a, t in zip(arrays, types)],
    )(*arrays)


def local(
    query_short,
    key_short,
    value_short,
    short_taps,
    query_long,
    key_long,
    long_residue,
    long_rate,
    cotangent,
):
    count = lax.axis_size("ctx")
    tokens_here, channels = query_short.shape
    modes = long_rate.shape[0]
    sequence = tokens_here * count
    planes = count // 4
    rows = count // ROW
    own_lanes = channels // ROW

    forward = forward_table()
    inputs = {
        "key_short": key_short,
        "value_short": value_short,
        "long_rate": long_rate,
        "query_long": query_long,
        "cotangent": cotangent,
        "long_residue": long_residue,
        "forward_three": jnp.asarray(three_terms(forward[:, :T])),
        "inverse_low": jnp.asarray(three_terms(inverse_table(np.arange(T)))),
        "short_taps": short_taps,
        "key_long": key_long,
        "query_short": query_short,
        "forward_two": jnp.asarray(two_terms(forward[:, :T])),
        "forward_full": jnp.asarray(two_terms(forward)),
        "inverse_high": jnp.asarray(three_terms(inverse_table(np.arange(T) + T))),
        "inverse_lags": jnp.asarray(three_terms(inverse_table(T - np.arange(T)))),
    }
    tokens = (tokens_here, channels)
    outputs = {
        "core_output": (tokens, BF16),
        "query_short_grad": (tokens, BF16),
        "key_short_grad": (tokens, BF16),
        "value_short_grad": (tokens, BF16),
        "query_long_grad": (tokens, BF16),
        "key_long_grad": (tokens, BF16),
        "taps_grad": (short_taps.shape, BF16),
    }
    scratch = {name: pltpu.VMEM(array.shape, array.dtype) for name, array in inputs.items()}
    scratch["load_sems"] = pltpu.SemaphoreType.DMA((len(inputs),))
    state = (modes, own_lanes)
    for name in ("later", "earlier"):
        for part in ("sums", "row", "local", "out", "got"):
            scratch[name + "_" + part] = pltpu.VMEM((ROW,) + state, F32)
        scratch[name + "_total"] = pltpu.VMEM(state, F32)
        scratch[name + "_rows"] = pltpu.VMEM((rows,) + state, F32)
        scratch[name + "_sems"] = pltpu.SemaphoreType.DMA((4,))
        scratch[name + "_row_sems"] = pltpu.SemaphoreType.DMA((2, rows))
    scratch["extended"] = pltpu.VMEM((2 * T, channels), BF16)
    scratch["back_ext"] = pltpu.VMEM((2 * T, channels), BF16)
    scratch["long_grad"] = pltpu.VMEM(tokens, BF16)
    scratch["long_input"] = pltpu.VMEM(tokens, BF16)
    scratch["long_part"] = pltpu.VMEM(tokens, F32)
    scratch["block_scr"] = pltpu.VMEM((T, WIDTH), F32)
    for name in ("filter_spec", "taps_spec", "input_spec", "own_spec"):
        scratch[name] = pltpu.VMEM((N, channels), F32)
    scratch["lags"] = pltpu.VMEM((T, channels), F32)
    scratch["half_scr"] = pltpu.VMEM((T, channels // 2), F32)
    tile = (2 * T // planes, channels // 4)
    scratch["sum_scr"] = pltpu.VMEM((planes,) + tile, BF16)
    scratch["plane_scr"] = pltpu.VMEM((planes,) + tile, BF16)
    scratch["own_scr"] = pltpu.VMEM(tile, F32)
    scratch["pair_scr"] = pltpu.VMEM(tile, F32)
    for name in ("front", "behind"):
        for part in ("_held", "_passed"):
            scratch[name + part] = pltpu.VMEM((T, channels // ROW), BF16)
        scratch[name + "_sems"] = pltpu.SemaphoreType.DMA((7,))
    scratch["lag_sems"] = pltpu.SemaphoreType.DMA((2, 5))

    names = [name + "_hbm" for name in inputs] + list(outputs) + list(scratch)
    results = pl.pallas_call(
        functools.partial(
            core_kernel,
            names=tuple(names),
            loads=tuple(inputs),
            count=count,
            scale=sequence**-0.5,
        ),
        in_specs=[pl.BlockSpec(memory_space=pltpu.HBM)] * len(inputs),
        out_specs=[pl.BlockSpec(memory_space=pltpu.VMEM)] * len(outputs),
        out_shape=[jax.ShapeDtypeStruct(shape, dtype) for shape, dtype in outputs.values()],
        scratch_shapes=list(scratch.values()),
        compiler_params=pltpu.CompilerParams(
            collective_id=0, has_side_effects=True, vmem_limit_bytes=VMEM_LIMIT
        ),
    )(*inputs.values())
    return tuple(stored(results, [BF16] * (len(outputs) - 1) + [F32]))


def solution(mesh):
    tokens = P("ctx", "ch")
    table = P(None, "ch")
    return jax.shard_map(
        local,
        mesh=mesh,
        in_specs=(tokens, tokens, tokens, table, tokens, tokens, table, table, tokens),
        out_specs=(tokens, tokens, tokens, tokens, tokens, tokens, table),
        check_vma=False,
    )
```

```python
import functools
import types

import jax
import jax.numpy as jnp
import ml_dtypes
import numpy as np
from jax import lax
from jax.experimental import pallas as pl
from jax.experimental.pallas import tpu as pltpu
from jax.sharding import PartitionSpec as P

F32 = jnp.float32
BF16 = jnp.bfloat16
T = 128
N = 2 * T
LANES = 128
VMEM_LIMIT = 63 * 1024 * 1024
CHIPS_X = 4
ROW = 2 * CHIPS_X
WIDTH = 512
MESH = pl.DeviceIdType.MESH


def forward_table():
    n = np.arange(N)
    k = np.arange(T)
    angle = 2.0 * np.pi * ((k[:, None] * n[None, :]) % N) / N
    low = -np.sin(angle)
    low[0] = (-1.0) ** n
    return np.concatenate([np.cos(angle), low], axis=0)


def inverse_table(rows):
    n = np.asarray(rows)
    k = np.arange(T)
    angle = 2.0 * np.pi * ((n[:, None] * k[None, :]) % N) / N
    weight = np.full((T,), 2.0 / N)
    weight[0] = 1.0 / N
    low = -np.sin(angle) * weight
    low[:, 0] = (-1.0) ** n / N
    return np.concatenate([np.cos(angle) * weight, low], axis=1)


def halves(table):
    high = table.astype(ml_dtypes.bfloat16)
    low = (table - high.astype(np.float64)).astype(ml_dtypes.bfloat16)
    return high, low


def two_terms(table):
    high, low = halves(table)
    return np.concatenate([high, low], axis=1)


def three_terms(table):
    high, low = halves(table)
    return np.concatenate([high, low, high], axis=1)


def dot(table, data):
    return jnp.dot(table, data, preferred_element_type=F32)


def exact(data):
    return jnp.concatenate([data, data], axis=0)


def split(data):
    high = data.astype(BF16)
    low = (data - high.astype(F32)).astype(BF16)
    return jnp.concatenate([high, high, low], axis=0)


def product(first, second, conjugate):
    ar, ai = first[:T], first[T:]
    br, bi = second[:T], second[T:]
    top = lax.broadcasted_iota(jnp.int32, ar.shape, 0) == 0
    rr, ii = ar * br, ai * bi
    if conjugate:
        re = rr + jnp.where(top, 0.0, ii)
        im = jnp.where(top, ii, ai * br - ar * bi)
    else:
        re = rr - jnp.where(top, 0.0, ii)
        im = jnp.where(top, ii, ai * br + ar * bi)
    return jnp.concatenate([re, im], axis=0)


def rows_iota():
    return lax.broadcasted_iota(jnp.int32, (8, LANES), 0).astype(F32)


def state_sums(tiles, steps_ref, ends_ref, lanes):
    rows = []
    for m in range(steps_ref.shape[0]):
        step = steps_ref[m, :, lanes]
        total = tiles[0]
        for tile in tiles[1:]:
            total = total * step + tile
        rows.append(jnp.sum(total * ends_ref[m, :, lanes], axis=0, keepdims=True))
    return rows


def mode_series(out_ref, out_lanes, scales, steps_ref, ends_ref, lanes, rising):
    modes = range(steps_ref.shape[0])
    steps = [steps_ref[m, :, lanes] for m in modes]
    terms = [scales[m : m + 1] * ends_ref[m, :, lanes] for m in modes]
    order = range(T // 8) if rising else range(T // 8 - 1, -1, -1)
    for place, q in enumerate(order):
        if place:
            terms = [term * step for term, step in zip(terms, steps)]
        layer = terms
        while len(layer) > 1:
            layer = [layer[i] + layer[i + 1] for i in range(0, len(layer), 2)]
        out_ref[8 * q : 8 * q + 8, out_lanes] = layer[0]


def send(source, target, peer, send_sem, recv_sem):
    copy = pltpu.make_async_remote_copy(
        src_ref=source,
        dst_ref=target,
        send_sem=send_sem,
        recv_sem=recv_sem,
        device_id={"ctx": peer},
        device_id_type=MESH,
    )
    copy.start()
    return copy


def wait_bytes(ref, sem):
    pltpu.make_async_copy(ref, ref, sem).wait()


def each_peer(count, body):
    for i in range(1, count):
        body(i)


def each(low, high, body):
    lax.fori_loop(low, high, lambda i, _: (body(i), 0)[1], 0)


class Place:
    def __init__(self, count):
        self.count = count
        self.me = lax.axis_index("ctx")
        self.core = lax.rem(self.me, 2)
        self.along_x = lax.rem(self.me // 2, CHIPS_X)
        self.in_row = lax.rem(self.me, ROW)
        self.row = self.me // ROW
        self.far = lax.rem(self.row, 2)
        self.along_y = self.row // 2
        self.rows = count // ROW
        self.planes = count // 4
        self.spot = self.along_y * CHIPS_X + self.along_x
        self.sibling = self.me + 1 - 2 * self.core
        self.partner = self.me + ROW * (1 - 2 * self.far)

    def row_peer(self, i):
        return lax.rem(self.in_row + i, ROW)

    def plane_device(self, spot):
        return (spot // CHIPS_X * 2 + self.far) * ROW + lax.rem(spot, CHIPS_X) * 2 + self.core


def greet(here):
    barrier = pltpu.get_barrier_semaphore()

    def signal(device):
        pl.semaphore_signal(barrier, inc=1, device_id={"ctx": device}, device_id_type=MESH)

    each_peer(ROW, lambda i: signal(here.row * ROW + here.row_peer(i)))
    each_peer(here.rows, lambda i: signal(lax.rem(here.row + i, here.rows) * ROW + here.in_row))
    chips_y = here.rows // 2
    for i in range(1, CHIPS_X):
        for j in range(1, chips_y):
            spot = lax.rem(here.along_y + j, chips_y) * CHIPS_X + lax.rem(
                here.along_x + i, CHIPS_X
            )
            signal(here.plane_device(spot))
    signal(lax.rem(here.me + 1, here.count))
    signal(lax.rem(here.me + here.count - 1, here.count))
    greeted = ROW - 1 + here.rows - 1 + (CHIPS_X - 1) * (chips_y - 1) + 2

    def finish():
        pl.semaphore_wait(barrier, greeted)

    return finish


class Carry:
    def __init__(self, here, refs, name, later, rate_ref):
        self.here, self.later, self.rate_ref = here, later, rate_ref
        for part in ("sums", "row", "local", "total", "rows", "out", "got", "sems", "row_sems"):
            setattr(self, part, getattr(refs, name + "_" + part))
        self.peers = pl.ds(0, ROW - 1)

    def to_row(self, source, target, send_sem, recv_sem):
        here = self.here

        def body(i):
            peer = here.row_peer(i)
            send(
                source.at[peer], target.at[here.in_row], here.row * ROW + peer, send_sem, recv_sem
            )

        each_peer(ROW, body)
        target[here.in_row] = source[here.in_row]

    def step(self):
        lanes = self.got.shape[2]
        own = pl.ds(pl.multiple_of(self.here.in_row * lanes, LANES), lanes)
        return self.rate_ref[:, own]

    def order(self):
        return range(ROW - 1, -1, -1) if self.later else range(ROW)

    def first(self):
        self.to_row(self.sums, self.row, self.sems.at[0], self.sems.at[1])

    def column_ranges(self):
        row, rows = self.here.row, self.here.rows
        after, before = (row + 1, rows), (0, row)
        return (before, after) if self.later else (after, before)

    def second(self):
        here = self.here
        wait_bytes(self.row.at[self.peers], self.sems.at[1])
        step = jnp.exp(-float(T) * self.step())
        carry = jnp.zeros(step.shape, F32)
        for k in self.order():
            self.local[k] = carry
            carry = carry * step + self.row[k]
        self.total[...] = carry
        targets, _ = self.column_ranges()
        each(
            *targets,
            lambda k: send(
                self.total,
                self.rows.at[here.row],
                k * ROW + here.in_row,
                self.row_sems.at[0, k],
                self.row_sems.at[1, here.row],
            ),
        )

    def third(self):
        here = self.here
        _, (low, high) = self.column_ranges()
        each(low, high, lambda k: wait_bytes(self.total, self.row_sems.at[1, k]))
        rate = self.step()
        leap = jnp.exp(-float(T * ROW) * rate)

        def body(i, carry):
            k = high - 1 - (i - low) if self.later else i
            return carry * leap + self.rows[k]

        carry = lax.fori_loop(low, high, body, jnp.zeros(rate.shape, F32))
        step = jnp.exp(-float(T) * rate)
        for k in self.order():
            self.out[k] = self.local[k] + carry
            carry = carry * step
        self.to_row(self.out, self.got, self.sems.at[2], self.sems.at[3])

    def arrive(self):
        wait_bytes(self.got.at[self.peers], self.sems.at[3])

    def settle(self):
        targets, _ = self.column_ranges()
        wait_bytes(self.sums.at[self.peers], self.sems.at[0])
        each(*targets, lambda k: wait_bytes(self.total, self.row_sems.at[0, k]))
        wait_bytes(self.out.at[self.peers], self.sems.at[2])


class Halo:
    def __init__(self, here, buffer, source_rows, target_rows, onward, relays, sems):
        self.here, self.sems = here, sems
        self.source, self.target = buffer.at[source_rows], buffer.at[target_rows]
        self.held, self.passed = relays
        self.step = 1 if onward else -1
        first, last = here.in_row == 0, here.in_row == ROW - 1
        low, high = here.row > 0, here.row < here.rows - 1
        self.leaves, self.enters = (last, first) if onward else (first, last)
        self.sends_row, self.takes_row = (high, low) if onward else (low, high)
        self.entry = 0 if onward else ROW - 1
        self.piece = buffer.shape[1] // ROW

    def lanes(self, j):
        return pl.ds(pl.multiple_of(j * self.piece, self.piece), self.piece)

    def first(self):
        here, sems = self.here, self.sems

        @pl.when(jnp.logical_not(self.leaves))
        def _():
            send(self.source, self.target, here.me + self.step, sems.at[0], sems.at[1])

        @pl.when(self.leaves & self.sends_row)
        def _():
            def body(i):
                j = here.row_peer(i)
                send(
                    self.source.at[:, self.lanes(j)],
                    self.held,
                    here.row * ROW + j,
                    sems.at[2],
                    sems.at[3],
                )

            each_peer(ROW, body)

    def second(self):
        here, sems = self.here, self.sems
        over = here.me + self.step * ROW
        own = self.lanes(here.in_row)

        @pl.when(self.sends_row & self.leaves)
        def _():
            send(self.source.at[:, own], self.passed, over, sems.at[4], sems.at[5])

        @pl.when(self.sends_row & jnp.logical_not(self.leaves))
        def _():
            wait_bytes(self.held, sems.at[3])

        @pl.when(self.sends_row & self.enters)
        def _():
            send(self.held, self.target.at[:, own], over, sems.at[4], sems.at[1])

        @pl.when(self.sends_row & jnp.logical_not(self.enters | self.leaves))
        def _():
            send(self.held, self.passed, over, sems.at[4], sems.at[5])

    def third(self):
        here, sems = self.here, self.sems

        @pl.when(self.takes_row & jnp.logical_not(self.enters))
        def _():
            wait_bytes(self.passed, sems.at[5])
            send(
                self.passed,
                self.target.at[:, self.lanes(here.in_row)],
                here.row * ROW + self.entry,
                sems.at[6],
                sems.at[1],
            )

    def arrive(self):
        @pl.when(self.takes_row | jnp.logical_not(self.enters))
        def _():
            wait_bytes(self.target, self.sems.at[1])

    def settle(self):
        sems = self.sems

        @pl.when(jnp.logical_not(self.leaves))
        def _():
            wait_bytes(self.source, sems.at[0])

        @pl.when(self.leaves & self.sends_row)
        def _():
            wait_bytes(self.source.at[:, pl.ds(0, (ROW - 1) * self.piece)], sems.at[2])

        @pl.when(self.sends_row)
        def _():
            wait_bytes(self.held, sems.at[4])

        @pl.when(self.takes_row & jnp.logical_not(self.enters))
        def _():
            wait_bytes(self.passed, sems.at[6])


def put_states(out_ref, block, group, rows):
    half = group % 2 * LANES
    for m, row in enumerate(rows):
        out_ref[block * (WIDTH // 256) + group // 2, m : m + 1, half : half + LANES] = row


def take_scales(states_ref, block, group, residue):
    half = group % 2 * LANES
    return residue * states_ref[block * (WIDTH // 256) + group // 2, :, half : half + LANES]


def core_kernel(*refs, names, loads, count, scale):
    r = types.SimpleNamespace(**dict(zip(names, refs)))
    here = Place(count)
    channels = r.long_rate.shape[1]
    blocks = channels // WIDTH
    groups = WIDTH // LANES

    copies = {
        name: pltpu.make_async_copy(getattr(r, name + "_hbm"), getattr(r, name), r.load_sems.at[k])
        for k, name in enumerate(loads)
    }
    met = greet(here)
    for name in loads:
        copies[name].start()
    leaving = []

    def leave(*done):
        for name in done:
            copy = pltpu.make_async_copy(
                getattr(r, name), getattr(r, name + "_out"), r.store_sems.at[len(leaving)]
            )
            copy.start()
            leaving.append(copy)

    def need(*wanted):
        for name in wanted:
            copies[name].wait()

    def cols(block):
        return pl.ds(pl.multiple_of(block * WIDTH, WIDTH), WIDTH)

    def lanes_of(block, group):
        return pl.ds(pl.multiple_of(block * WIDTH + group * LANES, LANES), LANES)

    def wide(ref, block):
        return ref[:, cols(block)].astype(F32)

    need("long_rate", "query_long", "cotangent")
    iota = rows_iota()

    def make_tables(b):
        for group in range(groups):
            lanes = lanes_of(b, group)
            for m in range(r.long_rate.shape[0]):
                rate = jnp.broadcast_to(r.long_rate[m : m + 1, lanes], (8, LANES))
                r.steps[m, :, lanes] = jnp.exp(-8.0 * rate)
                r.rise[m, :, lanes] = jnp.exp(-rate * iota)
                r.fall[m, :, lanes] = jnp.exp(-rate * (7.0 - iota))

    each(0, blocks, make_tables)

    def make_back_states(b):
        for group in range(groups):
            lanes = lanes_of(b, group)
            back = r.query_long[:, lanes].astype(F32) * r.cotangent[:, lanes].astype(F32)
            tiles = [back[8 * q : 8 * q + 8] for q in range(T // 8 - 1, -1, -1)]
            put_states(r.later_sums, b, group, state_sums(tiles, r.steps, r.rise, lanes))

    each(0, blocks, make_back_states)

    need("key_short", "value_short")

    def make_short_input(b):
        r.extended[T:, cols(b)] = (wide(r.key_short, b) * wide(r.value_short, b)).astype(BF16)

    each(0, blocks, make_short_input)
    last = count - 1
    own_rows, before_rows = pl.ds(T, T), pl.ds(0, T)
    front = Halo(
        here, r.extended, own_rows, before_rows, True, (r.front_held, r.front_passed), r.front_sems
    )
    behind = Halo(
        here,
        r.back_ext,
        before_rows,
        own_rows,
        False,
        (r.behind_held, r.behind_passed),
        r.behind_sems,
    )

    @pl.when(here.me == 0)
    def _():
        r.extended[:T] = jnp.zeros((T, channels), BF16)

    @pl.when(here.me == last)
    def _():
        r.back_ext[T:] = jnp.zeros((T, channels), BF16)

    later = Carry(here, r, "later", True, r.long_rate)
    met()
    later.first()
    front.first()

    need("long_residue", "forward_three")

    def make_filter(b):
        for group in range(groups):
            lanes = lanes_of(b, group)
            own = pl.ds(group * LANES, LANES)
            scales = r.long_residue[:, lanes]
            mode_series(r.block_scr, own, scales, r.steps, r.rise, lanes, True)
        r.filter_spec[:, cols(b)] = dot(r.forward_three[...], split(r.block_scr[...]))

    each(0, blocks, make_filter)
    later.second()
    front.second()

    need("inverse_low", "short_taps")

    def make_local_grad(b):
        back = wide(r.query_long, b) * wide(r.cotangent, b)
        spectrum = dot(r.forward_three[...], split(back))
        turned = product(spectrum, r.filter_spec[:, cols(b)], True)
        r.long_part[:, cols(b)] = dot(r.inverse_low[...], split(turned))
        r.taps_spec[:, cols(b)] = dot(r.forward_three[...], split(r.short_taps[:, cols(b)]))

    each(0, blocks, make_local_grad)
    later.third()
    front.third()
    need("key_long", "query_short", "forward_two")
    later.arrive()

    def make_long_grad(b):
        for group in range(groups):
            lanes = lanes_of(b, group)
            own = pl.ds(group * LANES, LANES)
            residue = r.long_residue[:, lanes] * jnp.exp(-r.long_rate[:, lanes])
            scales = take_scales(r.later_got, b, group, residue)
            mode_series(r.block_scr, own, scales, r.steps, r.fall, lanes, False)
        grad = (r.long_part[:, cols(b)] + r.block_scr[...]).astype(BF16)
        r.long_grad[:, cols(b)] = grad
        hidden_grad = grad.astype(F32) * wide(r.key_long, b)
        r.back_ext[:T, cols(b)] = (hidden_grad * wide(r.query_short, b)).astype(BF16)

    each(0, blocks, make_long_grad)
    behind.first()

    need("forward_full", "inverse_high", "inverse_lags")

    def own_spectrum(b):
        r.own_spec[:, cols(b)] = dot(r.forward_two[...], exact(r.back_ext[:T, cols(b)]))

    each(0, blocks, own_spectrum)
    front.arrive()
    half = channels // 2
    mine = pl.ds(pl.multiple_of(here.core * half, LANES), half)
    theirs = pl.ds(pl.multiple_of((1 - here.core) * half, LANES), half)

    def make_lags(b):
        spectrum = dot(r.forward_full[...], exact(r.extended[:, cols(b)]))
        r.input_spec[:, cols(b)] = spectrum
        turned = product(spectrum, r.own_spec[:, cols(b)], True)
        r.lags[:, cols(b)] = dot(r.inverse_lags[...], split(turned))

    each(0, blocks, make_lags)
    to_sibling = send(
        r.lags.at[:, theirs], r.half_scr, here.sibling, r.lag_sems.at[0, 0], r.lag_sems.at[1, 0]
    )
    behind.second()

    def make_hidden(b):
        turned = product(r.input_spec[:, cols(b)], r.taps_spec[:, cols(b)], False)
        short_mix = dot(r.inverse_high[...], split(turned))
        hidden = (wide(r.query_short, b) * short_mix).astype(BF16).astype(F32)
        key, grad = wide(r.key_long, b), wide(r.long_grad, b)
        r.key_long_grad[:, cols(b)] = (grad * hidden).astype(BF16)
        r.query_short_grad[:, cols(b)] = (grad * key * short_mix).astype(BF16)
        long_input = (key * hidden).astype(BF16)
        r.long_input[:, cols(b)] = long_input
        r.block_scr[...] = long_input.astype(F32)
        for group in range(groups):
            own = pl.ds(group * LANES, LANES)
            tiles = [r.block_scr[8 * q : 8 * q + 8, own] for q in range(T // 8)]
            rows = state_sums(tiles, r.steps, r.fall, lanes_of(b, group))
            put_states(r.earlier_sums, b, group, rows)

    to_sibling.wait()
    summed = r.lags[:, mine] + r.half_scr[...]
    tile_rows, tile_lanes = r.own_scr.shape
    for spot in range(here.planes):
        top, left = spot // 2 * tile_rows, spot % 2 * tile_lanes
        r.sum_scr[spot] = summed[top : top + tile_rows, left : left + tile_lanes].astype(BF16)

    def to_plane(i):
        spot = lax.rem(here.spot + i, here.planes)
        send(
            r.sum_scr.at[spot],
            r.plane_scr.at[here.spot],
            here.plane_device(spot),
            r.lag_sems.at[0, 1],
            r.lag_sems.at[1, 1],
        )

    each_peer(here.planes, to_plane)
    r.plane_scr[here.spot] = r.sum_scr[here.spot]

    each(0, blocks, make_hidden)
    leave("query_short_grad", "key_long_grad")
    earlier = Carry(here, r, "earlier", False, r.long_rate)
    earlier.first()
    behind.third()

    plane_rest = pl.ds(0, here.planes - 1)
    wait_bytes(r.plane_scr.at[plane_rest], r.lag_sems.at[1, 1])
    total = r.plane_scr[0].astype(F32)
    for spot in range(1, here.planes):
        total = total + r.plane_scr[spot].astype(F32)
    r.own_scr[...] = total
    to_partner = send(
        r.own_scr, r.pair_scr, here.partner, r.lag_sems.at[0, 2], r.lag_sems.at[1, 2]
    )
    earlier.second()

    def make_local_mix(b):
        spectrum = dot(r.forward_two[...], exact(r.long_input[:, cols(b)]))
        turned = product(spectrum, r.filter_spec[:, cols(b)], False)
        r.long_part[:, cols(b)] = dot(r.inverse_low[...], split(turned))

    each(0, blocks, make_local_mix)
    earlier.third()

    to_partner.wait()
    my_rows = pl.ds(pl.multiple_of(here.spot // 2 * tile_rows, tile_rows), tile_rows)
    my_lanes = pl.ds(
        pl.multiple_of(here.core * half + lax.rem(here.spot, 2) * tile_lanes, tile_lanes),
        tile_lanes,
    )
    r.taps_grad[my_rows, my_lanes] = ((r.own_scr[...] + r.pair_scr[...]) * scale).astype(BF16)

    def from_plane(i):
        spot = lax.rem(here.spot + i, here.planes)
        send(
            r.taps_grad.at[my_rows, my_lanes],
            r.taps_grad.at[my_rows, my_lanes],
            here.plane_device(spot),
            r.lag_sems.at[0, 3],
            r.lag_sems.at[1, 3],
        )

    each_peer(here.planes, from_plane)
    earlier.arrive()

    def make_core(b):
        for group in range(groups):
            lanes = lanes_of(b, group)
            own = pl.ds(group * LANES, LANES)
            residue = r.long_residue[:, lanes] * jnp.exp(-r.long_rate[:, lanes])
            scales = take_scales(r.earlier_got, b, group, residue)
            mode_series(r.block_scr, own, scales, r.steps, r.rise, lanes, True)
        long_mix = r.long_part[:, cols(b)] + r.block_scr[...]
        r.core_output[:, cols(b)] = (wide(r.query_long, b) * long_mix).astype(BF16)
        r.query_long_grad[:, cols(b)] = (wide(r.cotangent, b) * long_mix).astype(BF16)

    each(0, blocks, make_core)
    leave("core_output", "query_long_grad")

    behind.arrive()

    def make_short_grads(b):
        back = dot(r.forward_full[...], exact(r.back_ext[:, cols(b)]))
        turned = product(back, r.taps_spec[:, cols(b)], True)
        input_grad = dot(r.inverse_low[...], split(turned))
        r.key_short_grad[:, cols(b)] = (input_grad * wide(r.value_short, b)).astype(BF16)
        r.value_short_grad[:, cols(b)] = (input_grad * wide(r.key_short, b)).astype(BF16)

    each(0, blocks, make_short_grads)
    leave("key_short_grad", "value_short_grad")

    wait_bytes(r.plane_scr.at[plane_rest], r.lag_sems.at[1, 3])
    send(
        r.taps_grad.at[:, mine],
        r.taps_grad.at[:, mine],
        here.sibling,
        r.lag_sems.at[0, 4],
        r.lag_sems.at[1, 4],
    ).wait()
    leave("taps_grad")

    later.settle()
    earlier.settle()
    wait_bytes(r.sum_scr.at[plane_rest], r.lag_sems.at[0, 1])
    wait_bytes(r.sum_scr.at[plane_rest], r.lag_sems.at[0, 3])

    front.settle()
    behind.settle()
    for copy in leaving:
        copy.wait()


def store_kernel(*refs, count):
    sources, targets = refs[:count], refs[count : 2 * count]
    held = refs[2 * count : 3 * count]
    wide_scr, in_sems, out_sems = refs[3 * count :]
    incoming = [
        pltpu.make_async_copy(sources[k], held[k], in_sems.at[k]) for k in range(count)
    ]
    for copy in reversed(incoming):
        copy.start()
    outgoing = [
        pltpu.make_async_copy(held[k], targets[k], out_sems.at[k]) for k in range(count - 1)
    ]
    outgoing.append(pltpu.make_async_copy(wide_scr, targets[-1], out_sems.at[count - 1]))
    for k in reversed(range(count)):
        incoming[k].wait()
        if k == count - 1:
            wide_scr[...] = held[k][...].astype(F32)
        outgoing[k].start()
    for copy in outgoing:
        copy.wait()


def stored(arrays):
    count = len(arrays)
    types_out = [a.dtype for a in arrays[:-1]] + [F32]
    return pl.pallas_call(
        functools.partial(store_kernel, count=count),
        in_specs=[pl.BlockSpec(memory_space=pltpu.HBM)] * count,
        out_specs=[pl.BlockSpec(memory_space=pltpu.HBM)] * count,
        out_shape=[jax.ShapeDtypeStruct(a.shape, t) for a, t in zip(arrays, types_out)],
        scratch_shapes=[pltpu.VMEM(a.shape, a.dtype) for a in arrays]
        + [
            pltpu.VMEM(arrays[-1].shape, F32),
            pltpu.SemaphoreType.DMA((count,)),
            pltpu.SemaphoreType.DMA((count,)),
        ],
        compiler_params=pltpu.CompilerParams(vmem_limit_bytes=VMEM_LIMIT),
    )(*arrays)


def local(
    query_short,
    key_short,
    value_short,
    short_taps,
    query_long,
    key_long,
    long_residue,
    long_rate,
    cotangent,
):
    count = lax.axis_size("ctx")
    tokens_here, channels = query_short.shape
    modes = long_rate.shape[0]
    sequence = tokens_here * count
    planes = count // 4
    rows = count // ROW
    own_lanes = channels // ROW

    forward = forward_table()
    inputs = {
        "long_rate": long_rate,
        "query_long": query_long,
        "cotangent": cotangent,
        "key_short": key_short,
        "value_short": value_short,
        "long_residue": long_residue,
        "forward_three": jnp.asarray(three_terms(forward[:, :T])),
        "inverse_low": jnp.asarray(three_terms(inverse_table(np.arange(T)))),
        "short_taps": short_taps,
        "key_long": key_long,
        "query_short": query_short,
        "forward_two": jnp.asarray(two_terms(forward[:, :T])),
        "forward_full": jnp.asarray(two_terms(forward)),
        "inverse_high": jnp.asarray(three_terms(inverse_table(np.arange(T) + T))),
        "inverse_lags": jnp.asarray(three_terms(inverse_table(T - np.arange(T)))),
    }
    tokens = (tokens_here, channels)
    outputs = {
        "core_output": (tokens, BF16),
        "query_short_grad": (tokens, BF16),
        "key_short_grad": (tokens, BF16),
        "value_short_grad": (tokens, BF16),
        "query_long_grad": (tokens, BF16),
        "key_long_grad": (tokens, BF16),
        "taps_grad": (short_taps.shape, BF16),
    }
    scratch = {name: pltpu.VMEM(array.shape, array.dtype) for name, array in inputs.items()}
    for name, (shape, dtype) in outputs.items():
        scratch[name] = pltpu.VMEM(shape, dtype)
    for name in ("steps", "rise", "fall"):
        scratch[name] = pltpu.VMEM((modes, 8, channels), F32)
    scratch["store_sems"] = pltpu.SemaphoreType.DMA((len(outputs),))
    scratch["load_sems"] = pltpu.SemaphoreType.DMA((len(inputs),))
    state = (modes, own_lanes)
    for name in ("later", "earlier"):
        for part in ("sums", "row", "local", "out", "got"):
            scratch[name + "_" + part] = pltpu.VMEM((ROW,) + state, F32)
        scratch[name + "_total"] = pltpu.VMEM(state, F32)
        scratch[name + "_rows"] = pltpu.VMEM((rows,) + state, F32)
        scratch[name + "_sems"] = pltpu.SemaphoreType.DMA((4,))
        scratch[name + "_row_sems"] = pltpu.SemaphoreType.DMA((2, rows))
    scratch["extended"] = pltpu.VMEM((2 * T, channels), BF16)
    scratch["back_ext"] = pltpu.VMEM((2 * T, channels), BF16)
    scratch["long_grad"] = pltpu.VMEM(tokens, BF16)
    scratch["long_input"] = pltpu.VMEM(tokens, BF16)
    scratch["long_part"] = pltpu.VMEM(tokens, F32)
    scratch["block_scr"] = pltpu.VMEM((T, WIDTH), F32)
    for name in ("filter_spec", "taps_spec", "input_spec", "own_spec"):
        scratch[name] = pltpu.VMEM((N, channels), F32)
    scratch["lags"] = pltpu.VMEM((T, channels), F32)
    scratch["half_scr"] = pltpu.VMEM((T, channels // 2), F32)
    tile = (2 * T // planes, channels // 4)
    scratch["sum_scr"] = pltpu.VMEM((planes,) + tile, BF16)
    scratch["plane_scr"] = pltpu.VMEM((planes,) + tile, BF16)
    scratch["own_scr"] = pltpu.VMEM(tile, F32)
    scratch["pair_scr"] = pltpu.VMEM(tile, F32)
    for name in ("front", "behind"):
        for part in ("_held", "_passed"):
            scratch[name + part] = pltpu.VMEM((T, channels // ROW), BF16)
        scratch[name + "_sems"] = pltpu.SemaphoreType.DMA((7,))
    scratch["lag_sems"] = pltpu.SemaphoreType.DMA((2, 5))

    names = [name + "_hbm" for name in inputs] + [name + "_out" for name in outputs]
    names += list(scratch)
    results = pl.pallas_call(
        functools.partial(
            core_kernel,
            names=tuple(names),
            loads=tuple(inputs),
            count=count,
            scale=sequence**-0.5,
        ),
        in_specs=[pl.BlockSpec(memory_space=pltpu.HBM)] * len(inputs),
        out_specs=[pl.BlockSpec(memory_space=pltpu.HBM)] * len(outputs),
        out_shape=[jax.ShapeDtypeStruct(shape, dtype) for shape, dtype in outputs.values()],
        scratch_shapes=list(scratch.values()),
        compiler_params=pltpu.CompilerParams(
            collective_id=0, has_side_effects=True, vmem_limit_bytes=VMEM_LIMIT
        ),
    )(*inputs.values())
    return tuple(stored(results))


def solution(mesh):
    tokens = P("ctx", "ch")
    table = P(None, "ch")
    return jax.shard_map(
        local,
        mesh=mesh,
        in_specs=(tokens, tokens, tokens, table, tokens, tokens, table, table, tokens),
        out_specs=(tokens, tokens, tokens, tokens, tokens, tokens, table),
        check_vma=False,
    )
```

```python
import functools
import types

import jax
import jax.numpy as jnp
import ml_dtypes
import numpy as np
from jax import lax
from jax.experimental import pallas as pl
from jax.experimental.pallas import tpu as pltpu
from jax.sharding import PartitionSpec as P

F32 = jnp.float32
BF16 = jnp.bfloat16
T = 128
N = 2 * T
LANES = 128
VMEM_LIMIT = 63 * 1024 * 1024
CHIPS_X = 4
ROW = 2 * CHIPS_X
WIDTH = 512
MESH = pl.DeviceIdType.MESH


def forward_table():
    n = np.arange(N)
    k = np.arange(T)
    angle = 2.0 * np.pi * ((k[:, None] * n[None, :]) % N) / N
    low = -np.sin(angle)
    low[0] = (-1.0) ** n
    return np.concatenate([np.cos(angle), low], axis=0)


def inverse_table(rows):
    n = np.asarray(rows)
    k = np.arange(T)
    angle = 2.0 * np.pi * ((n[:, None] * k[None, :]) % N) / N
    weight = np.full((T,), 2.0 / N)
    weight[0] = 1.0 / N
    low = -np.sin(angle) * weight
    low[:, 0] = (-1.0) ** n / N
    return np.concatenate([np.cos(angle) * weight, low], axis=1)


def halves(table):
    high = table.astype(ml_dtypes.bfloat16)
    low = (table - high.astype(np.float64)).astype(ml_dtypes.bfloat16)
    return high, low


def two_terms(table):
    high, low = halves(table)
    return np.concatenate([high, low], axis=1)


def three_terms(table):
    high, low = halves(table)
    return np.concatenate([high, low, high], axis=1)


def dot(table, data):
    return jnp.dot(table, data, preferred_element_type=F32)


def exact(data):
    return jnp.concatenate([data, data], axis=0)


def split(data):
    high = data.astype(BF16)
    low = (data - high.astype(F32)).astype(BF16)
    return jnp.concatenate([high, high, low], axis=0)


def product(first, second, conjugate):
    ar, ai = first[:T], first[T:]
    br, bi = second[:T], second[T:]
    top = lax.broadcasted_iota(jnp.int32, ar.shape, 0) == 0
    rr, ii = ar * br, ai * bi
    if conjugate:
        re = rr + jnp.where(top, 0.0, ii)
        im = jnp.where(top, ii, ai * br - ar * bi)
    else:
        re = rr - jnp.where(top, 0.0, ii)
        im = jnp.where(top, ii, ai * br + ar * bi)
    return jnp.concatenate([re, im], axis=0)


def rows_iota():
    return lax.broadcasted_iota(jnp.int32, (8, LANES), 0).astype(F32)


def state_sums(tiles, steps_ref, ends_ref, lanes):
    rows = []
    for m in range(steps_ref.shape[0]):
        step = steps_ref[m, :, lanes]
        total = tiles[0]
        for tile in tiles[1:]:
            total = total * step + tile
        rows.append(jnp.sum(total * ends_ref[m, :, lanes], axis=0, keepdims=True))
    return rows


def mode_series(out_ref, out_lanes, scales, steps_ref, ends_ref, lanes, rising):
    modes = range(steps_ref.shape[0])
    steps = [steps_ref[m, :, lanes] for m in modes]
    terms = [scales[m : m + 1] * ends_ref[m, :, lanes] for m in modes]
    order = range(T // 8) if rising else range(T // 8 - 1, -1, -1)
    for place, q in enumerate(order):
        if place:
            terms = [term * step for term, step in zip(terms, steps)]
        layer = terms
        while len(layer) > 1:
            layer = [layer[i] + layer[i + 1] for i in range(0, len(layer), 2)]
        out_ref[8 * q : 8 * q + 8, out_lanes] = layer[0]


def send(source, target, peer, send_sem, recv_sem):
    copy = pltpu.make_async_remote_copy(
        src_ref=source,
        dst_ref=target,
        send_sem=send_sem,
        recv_sem=recv_sem,
        device_id={"ctx": peer},
        device_id_type=MESH,
    )
    copy.start()
    return copy


def wait_bytes(ref, sem):
    pltpu.make_async_copy(ref, ref, sem).wait()


def each_peer(count, body):
    for i in range(1, count):
        body(i)


def each(low, high, body):
    lax.fori_loop(low, high, lambda i, _: (body(i), 0)[1], 0)


class Place:
    def __init__(self, count):
        self.count = count
        self.me = lax.axis_index("ctx")
        self.core = lax.rem(self.me, 2)
        self.along_x = lax.rem(self.me // 2, CHIPS_X)
        self.in_row = lax.rem(self.me, ROW)
        self.row = self.me // ROW
        self.far = lax.rem(self.row, 2)
        self.along_y = self.row // 2
        self.rows = count // ROW
        self.planes = count // 4
        self.spot = self.along_y * CHIPS_X + self.along_x
        self.sibling = self.me + 1 - 2 * self.core
        self.partner = self.me + ROW * (1 - 2 * self.far)

    def row_peer(self, i):
        return lax.rem(self.in_row + i, ROW)

    def plane_device(self, spot):
        return (spot // CHIPS_X * 2 + self.far) * ROW + lax.rem(spot, CHIPS_X) * 2 + self.core


def greet(here):
    barrier = pltpu.get_barrier_semaphore()

    def signal(device):
        pl.semaphore_signal(barrier, inc=1, device_id={"ctx": device}, device_id_type=MESH)

    each_peer(ROW, lambda i: signal(here.row * ROW + here.row_peer(i)))
    each_peer(here.rows, lambda i: signal(lax.rem(here.row + i, here.rows) * ROW + here.in_row))
    chips_y = here.rows // 2
    for i in range(1, CHIPS_X):
        for j in range(1, chips_y):
            spot = lax.rem(here.along_y + j, chips_y) * CHIPS_X + lax.rem(
                here.along_x + i, CHIPS_X
            )
            signal(here.plane_device(spot))
    signal(lax.rem(here.me + 1, here.count))
    signal(lax.rem(here.me + here.count - 1, here.count))
    greeted = ROW - 1 + here.rows - 1 + (CHIPS_X - 1) * (chips_y - 1) + 2

    def finish():
        pl.semaphore_wait(barrier, greeted)

    return finish


class Carry:
    def __init__(self, here, refs, name, later, rate_ref):
        self.here, self.later, self.rate_ref = here, later, rate_ref
        for part in ("sums", "row", "local", "total", "rows", "out", "got", "sems", "row_sems"):
            setattr(self, part, getattr(refs, name + "_" + part))
        self.peers = pl.ds(0, ROW - 1)

    def to_row(self, source, target, send_sem, recv_sem):
        here = self.here

        def body(i):
            peer = here.row_peer(i)
            send(
                source.at[peer], target.at[here.in_row], here.row * ROW + peer, send_sem, recv_sem
            )

        each_peer(ROW, body)
        target[here.in_row] = source[here.in_row]

    def step(self):
        lanes = self.got.shape[2]
        own = pl.ds(pl.multiple_of(self.here.in_row * lanes, LANES), lanes)
        return self.rate_ref[:, own]

    def order(self):
        return range(ROW - 1, -1, -1) if self.later else range(ROW)

    def first(self):
        self.to_row(self.sums, self.row, self.sems.at[0], self.sems.at[1])

    def column_ranges(self):
        row, rows = self.here.row, self.here.rows
        after, before = (row + 1, rows), (0, row)
        return (before, after) if self.later else (after, before)

    def second(self):
        here = self.here
        wait_bytes(self.row.at[self.peers], self.sems.at[1])
        step = jnp.exp(-float(T) * self.step())
        carry = jnp.zeros(step.shape, F32)
        for k in self.order():
            self.local[k] = carry
            carry = carry * step + self.row[k]
        self.total[...] = carry
        targets, _ = self.column_ranges()
        each(
            *targets,
            lambda k: send(
                self.total,
                self.rows.at[here.row],
                k * ROW + here.in_row,
                self.row_sems.at[0, k],
                self.row_sems.at[1, here.row],
            ),
        )

    def third(self):
        here = self.here
        _, (low, high) = self.column_ranges()
        each(low, high, lambda k: wait_bytes(self.total, self.row_sems.at[1, k]))
        rate = self.step()
        leap = jnp.exp(-float(T * ROW) * rate)

        def body(i, carry):
            k = high - 1 - (i - low) if self.later else i
            return carry * leap + self.rows[k]

        carry = lax.fori_loop(low, high, body, jnp.zeros(rate.shape, F32))
        step = jnp.exp(-float(T) * rate)
        for k in self.order():
            self.out[k] = self.local[k] + carry
            carry = carry * step
        self.to_row(self.out, self.got, self.sems.at[2], self.sems.at[3])

    def arrive(self):
        wait_bytes(self.got.at[self.peers], self.sems.at[3])

    def settle(self):
        targets, _ = self.column_ranges()
        wait_bytes(self.sums.at[self.peers], self.sems.at[0])
        each(*targets, lambda k: wait_bytes(self.total, self.row_sems.at[0, k]))
        wait_bytes(self.out.at[self.peers], self.sems.at[2])


class Halo:
    def __init__(self, here, buffer, source_rows, target_rows, onward, relays, sems):
        self.here, self.sems = here, sems
        self.source, self.target = buffer.at[source_rows], buffer.at[target_rows]
        self.held, self.passed = relays
        self.step = 1 if onward else -1
        first, last = here.in_row == 0, here.in_row == ROW - 1
        low, high = here.row > 0, here.row < here.rows - 1
        self.leaves, self.enters = (last, first) if onward else (first, last)
        self.sends_row, self.takes_row = (high, low) if onward else (low, high)
        self.entry = 0 if onward else ROW - 1
        self.piece = buffer.shape[1] // ROW

    def lanes(self, j):
        return pl.ds(pl.multiple_of(j * self.piece, self.piece), self.piece)

    def near(self):
        here, sems = self.here, self.sems

        @pl.when(jnp.logical_not(self.leaves))
        def _():
            send(self.source, self.target, here.me + self.step, sems.at[0], sems.at[1])

    def first(self):
        here, sems = self.here, self.sems

        @pl.when(self.leaves & self.sends_row)
        def _():
            def body(i):
                j = here.row_peer(i)
                send(
                    self.source.at[:, self.lanes(j)],
                    self.held,
                    here.row * ROW + j,
                    sems.at[2],
                    sems.at[3],
                )

            each_peer(ROW, body)

    def second(self):
        here, sems = self.here, self.sems
        over = here.me + self.step * ROW
        own = self.lanes(here.in_row)

        @pl.when(self.sends_row & self.leaves)
        def _():
            send(self.source.at[:, own], self.passed, over, sems.at[4], sems.at[5])

        @pl.when(self.sends_row & jnp.logical_not(self.leaves))
        def _():
            wait_bytes(self.held, sems.at[3])

        @pl.when(self.sends_row & self.enters)
        def _():
            send(self.held, self.target.at[:, own], over, sems.at[4], sems.at[1])

        @pl.when(self.sends_row & jnp.logical_not(self.enters | self.leaves))
        def _():
            send(self.held, self.passed, over, sems.at[4], sems.at[5])

    def third(self):
        here, sems = self.here, self.sems

        @pl.when(self.takes_row & jnp.logical_not(self.enters))
        def _():
            wait_bytes(self.passed, sems.at[5])
            send(
                self.passed,
                self.target.at[:, self.lanes(here.in_row)],
                here.row * ROW + self.entry,
                sems.at[6],
                sems.at[1],
            )

    def arrive(self):
        @pl.when(self.takes_row | jnp.logical_not(self.enters))
        def _():
            wait_bytes(self.target, self.sems.at[1])

    def settle(self):
        sems = self.sems

        @pl.when(jnp.logical_not(self.leaves))
        def _():
            wait_bytes(self.source, sems.at[0])

        @pl.when(self.leaves & self.sends_row)
        def _():
            wait_bytes(self.source.at[:, pl.ds(0, (ROW - 1) * self.piece)], sems.at[2])

        @pl.when(self.sends_row)
        def _():
            wait_bytes(self.held, sems.at[4])

        @pl.when(self.takes_row & jnp.logical_not(self.enters))
        def _():
            wait_bytes(self.passed, sems.at[6])


def put_states(out_ref, block, group, rows):
    half = group % 2 * LANES
    for m, row in enumerate(rows):
        out_ref[block * (WIDTH // 256) + group // 2, m : m + 1, half : half + LANES] = row


def take_scales(states_ref, block, group, residue):
    half = group % 2 * LANES
    return residue * states_ref[block * (WIDTH // 256) + group // 2, :, half : half + LANES]


def core_kernel(*refs, names, loads, count, scale):
    r = types.SimpleNamespace(**dict(zip(names, refs)))
    here = Place(count)
    channels = r.long_rate.shape[1]
    blocks = channels // WIDTH
    groups = WIDTH // LANES

    copies = {
        name: pltpu.make_async_copy(getattr(r, name + "_hbm"), getattr(r, name), r.load_sems.at[k])
        for k, name in enumerate(loads)
    }
    met = greet(here)
    for name in loads:
        copies[name].start()
    leaving = []

    def leave(*done):
        for name in done:
            copy = pltpu.make_async_copy(
                getattr(r, name), getattr(r, name + "_out"), r.store_sems.at[len(leaving)]
            )
            copy.start()
            leaving.append(copy)

    def need(*wanted):
        for name in wanted:
            copies[name].wait()

    def cols(block):
        return pl.ds(pl.multiple_of(block * WIDTH, WIDTH), WIDTH)

    def lanes_of(block, group):
        return pl.ds(pl.multiple_of(block * WIDTH + group * LANES, LANES), LANES)

    def wide(ref, block):
        return ref[:, cols(block)].astype(F32)

    need("long_rate", "query_long", "cotangent")
    iota = rows_iota()

    def make_tables(b):
        for group in range(groups):
            lanes = lanes_of(b, group)
            for m in range(r.long_rate.shape[0]):
                rate = jnp.broadcast_to(r.long_rate[m : m + 1, lanes], (8, LANES))
                r.steps[m, :, lanes] = jnp.exp(-8.0 * rate)
                r.rise[m, :, lanes] = jnp.exp(-rate * iota)
                r.fall[m, :, lanes] = jnp.exp(-rate * (7.0 - iota))

    each(0, blocks, make_tables)

    def make_back_states(b):
        for group in range(groups):
            lanes = lanes_of(b, group)
            back = r.query_long[:, lanes].astype(F32) * r.cotangent[:, lanes].astype(F32)
            tiles = [back[8 * q : 8 * q + 8] for q in range(T // 8 - 1, -1, -1)]
            put_states(r.later_sums, b, group, state_sums(tiles, r.steps, r.rise, lanes))

    each(0, blocks, make_back_states)

    need("key_short", "value_short")

    def make_short_input(b):
        r.extended[T:, cols(b)] = (wide(r.key_short, b) * wide(r.value_short, b)).astype(BF16)

    each(0, blocks, make_short_input)
    last = count - 1
    own_rows, before_rows = pl.ds(T, T), pl.ds(0, T)
    front = Halo(
        here, r.extended, own_rows, before_rows, True, (r.front_held, r.front_passed), r.front_sems
    )
    behind = Halo(
        here,
        r.back_ext,
        before_rows,
        own_rows,
        False,
        (r.behind_held, r.behind_passed),
        r.behind_sems,
    )

    @pl.when(here.me == 0)
    def _():
        r.extended[:T] = jnp.zeros((T, channels), BF16)

    @pl.when(here.me == last)
    def _():
        r.back_ext[T:] = jnp.zeros((T, channels), BF16)

    later = Carry(here, r, "later", True, r.long_rate)
    met()
    later.first()
    front.first()

    need("long_residue", "forward_three")

    def make_filter(b):
        for group in range(groups):
            lanes = lanes_of(b, group)
            own = pl.ds(group * LANES, LANES)
            scales = r.long_residue[:, lanes]
            mode_series(r.block_scr, own, scales, r.steps, r.rise, lanes, True)
        r.filter_spec[:, cols(b)] = dot(r.forward_three[...], split(r.block_scr[...]))

    each(0, blocks, make_filter)
    later.second()
    front.near()
    front.second()

    need("inverse_low", "short_taps")

    def make_local_grad(b):
        back = wide(r.query_long, b) * wide(r.cotangent, b)
        spectrum = dot(r.forward_three[...], split(back))
        turned = product(spectrum, r.filter_spec[:, cols(b)], True)
        r.long_part[:, cols(b)] = dot(r.inverse_low[...], split(turned))
        r.taps_spec[:, cols(b)] = dot(r.forward_three[...], split(r.short_taps[:, cols(b)]))

    each(0, blocks, make_local_grad)
    later.third()
    front.third()
    need("key_long", "query_short", "forward_two")
    later.arrive()

    def make_long_grad(b):
        for group in range(groups):
            lanes = lanes_of(b, group)
            own = pl.ds(group * LANES, LANES)
            residue = r.long_residue[:, lanes] * jnp.exp(-r.long_rate[:, lanes])
            scales = take_scales(r.later_got, b, group, residue)
            mode_series(r.block_scr, own, scales, r.steps, r.fall, lanes, False)
        grad = (r.long_part[:, cols(b)] + r.block_scr[...]).astype(BF16)
        r.long_grad[:, cols(b)] = grad
        hidden_grad = grad.astype(F32) * wide(r.key_long, b)
        r.back_ext[:T, cols(b)] = (hidden_grad * wide(r.query_short, b)).astype(BF16)

    each(0, blocks, make_long_grad)
    behind.near()
    behind.first()

    need("forward_full", "inverse_high", "inverse_lags")

    def own_spectrum(b):
        r.own_spec[:, cols(b)] = dot(r.forward_two[...], exact(r.back_ext[:T, cols(b)]))

    each(0, blocks, own_spectrum)
    front.arrive()
    half = channels // 2
    mine = pl.ds(pl.multiple_of(here.core * half, LANES), half)
    theirs = pl.ds(pl.multiple_of((1 - here.core) * half, LANES), half)

    def make_lags(b):
        spectrum = dot(r.forward_full[...], exact(r.extended[:, cols(b)]))
        r.input_spec[:, cols(b)] = spectrum
        turned = product(spectrum, r.own_spec[:, cols(b)], True)
        r.lags[:, cols(b)] = dot(r.inverse_lags[...], split(turned))

    each(0, blocks, make_lags)
    to_sibling = send(
        r.lags.at[:, theirs], r.half_scr, here.sibling, r.lag_sems.at[0, 0], r.lag_sems.at[1, 0]
    )
    behind.second()

    def make_hidden(b):
        turned = product(r.input_spec[:, cols(b)], r.taps_spec[:, cols(b)], False)
        short_mix = dot(r.inverse_high[...], split(turned))
        hidden = (wide(r.query_short, b) * short_mix).astype(BF16).astype(F32)
        key, grad = wide(r.key_long, b), wide(r.long_grad, b)
        r.key_long_grad[:, cols(b)] = (grad * hidden).astype(BF16)
        r.query_short_grad[:, cols(b)] = (grad * key * short_mix).astype(BF16)
        long_input = (key * hidden).astype(BF16)
        r.long_input[:, cols(b)] = long_input
        r.block_scr[...] = long_input.astype(F32)
        for group in range(groups):
            own = pl.ds(group * LANES, LANES)
            tiles = [r.block_scr[8 * q : 8 * q + 8, own] for q in range(T // 8)]
            rows = state_sums(tiles, r.steps, r.fall, lanes_of(b, group))
            put_states(r.earlier_sums, b, group, rows)

    to_sibling.wait()
    summed = r.lags[:, mine] + r.half_scr[...]
    tile_rows, tile_lanes = r.own_scr.shape
    for spot in range(here.planes):
        top, left = spot // 2 * tile_rows, spot % 2 * tile_lanes
        r.sum_scr[spot] = summed[top : top + tile_rows, left : left + tile_lanes].astype(BF16)

    def to_plane(i):
        spot = lax.rem(here.spot + i, here.planes)
        send(
            r.sum_scr.at[spot],
            r.plane_scr.at[here.spot],
            here.plane_device(spot),
            r.lag_sems.at[0, 1],
            r.lag_sems.at[1, 1],
        )

    each_peer(here.planes, to_plane)
    r.plane_scr[here.spot] = r.sum_scr[here.spot]

    each(0, blocks, make_hidden)
    leave("query_short_grad", "key_long_grad")
    earlier = Carry(here, r, "earlier", False, r.long_rate)
    earlier.first()
    behind.third()

    plane_rest = pl.ds(0, here.planes - 1)
    wait_bytes(r.plane_scr.at[plane_rest], r.lag_sems.at[1, 1])
    total = r.plane_scr[0].astype(F32)
    for spot in range(1, here.planes):
        total = total + r.plane_scr[spot].astype(F32)
    r.own_scr[...] = total
    to_partner = send(
        r.own_scr, r.pair_scr, here.partner, r.lag_sems.at[0, 2], r.lag_sems.at[1, 2]
    )
    earlier.second()

    def make_local_mix(b):
        spectrum = dot(r.forward_two[...], exact(r.long_input[:, cols(b)]))
        turned = product(spectrum, r.filter_spec[:, cols(b)], False)
        r.long_part[:, cols(b)] = dot(r.inverse_low[...], split(turned))

    each(0, blocks, make_local_mix)
    earlier.third()

    to_partner.wait()
    my_rows = pl.ds(pl.multiple_of(here.spot // 2 * tile_rows, tile_rows), tile_rows)
    my_lanes = pl.ds(
        pl.multiple_of(here.core * half + lax.rem(here.spot, 2) * tile_lanes, tile_lanes),
        tile_lanes,
    )
    r.taps_grad[my_rows, my_lanes] = ((r.own_scr[...] + r.pair_scr[...]) * scale).astype(BF16)

    def from_plane(i):
        spot = lax.rem(here.spot + i, here.planes)
        send(
            r.taps_grad.at[my_rows, my_lanes],
            r.taps_grad.at[my_rows, my_lanes],
            here.plane_device(spot),
            r.lag_sems.at[0, 3],
            r.lag_sems.at[1, 3],
        )

    each_peer(here.planes, from_plane)
    earlier.arrive()

    def make_core(b):
        for group in range(groups):
            lanes = lanes_of(b, group)
            own = pl.ds(group * LANES, LANES)
            residue = r.long_residue[:, lanes] * jnp.exp(-r.long_rate[:, lanes])
            scales = take_scales(r.earlier_got, b, group, residue)
            mode_series(r.block_scr, own, scales, r.steps, r.rise, lanes, True)
        long_mix = r.long_part[:, cols(b)] + r.block_scr[...]
        r.core_output[:, cols(b)] = (wide(r.query_long, b) * long_mix).astype(BF16)
        r.query_long_grad[:, cols(b)] = (wide(r.cotangent, b) * long_mix).astype(BF16)

    each(0, blocks, make_core)
    leave("core_output", "query_long_grad")

    behind.arrive()

    def make_short_grads(b):
        back = dot(r.forward_full[...], exact(r.back_ext[:, cols(b)]))
        turned = product(back, r.taps_spec[:, cols(b)], True)
        input_grad = dot(r.inverse_low[...], split(turned))
        r.key_short_grad[:, cols(b)] = (input_grad * wide(r.value_short, b)).astype(BF16)
        r.value_short_grad[:, cols(b)] = (input_grad * wide(r.key_short, b)).astype(BF16)

    each(0, blocks, make_short_grads)
    leave("key_short_grad", "value_short_grad")

    wait_bytes(r.plane_scr.at[plane_rest], r.lag_sems.at[1, 3])
    send(
        r.taps_grad.at[:, mine],
        r.taps_grad.at[:, mine],
        here.sibling,
        r.lag_sems.at[0, 4],
        r.lag_sems.at[1, 4],
    ).wait()
    leave("taps_grad")

    later.settle()
    earlier.settle()
    wait_bytes(r.sum_scr.at[plane_rest], r.lag_sems.at[0, 1])
    wait_bytes(r.sum_scr.at[plane_rest], r.lag_sems.at[0, 3])

    front.settle()
    behind.settle()
    for copy in leaving:
        copy.wait()


def store_kernel(*refs, count):
    sources, targets = refs[:count], refs[count : 2 * count]
    held = refs[2 * count : 3 * count]
    wide_scr, in_sems, out_sems = refs[3 * count :]
    incoming = [
        pltpu.make_async_copy(sources[k], held[k], in_sems.at[k]) for k in range(count)
    ]
    for copy in reversed(incoming):
        copy.start()
    outgoing = [
        pltpu.make_async_copy(held[k], targets[k], out_sems.at[k]) for k in range(count - 1)
    ]
    outgoing.append(pltpu.make_async_copy(wide_scr, targets[-1], out_sems.at[count - 1]))
    for k in reversed(range(count)):
        incoming[k].wait()
        if k == count - 1:
            wide_scr[...] = held[k][...].astype(F32)
        outgoing[k].start()
    for copy in outgoing:
        copy.wait()


def stored(arrays):
    count = len(arrays)
    types_out = [a.dtype for a in arrays[:-1]] + [F32]
    return pl.pallas_call(
        functools.partial(store_kernel, count=count),
        in_specs=[pl.BlockSpec(memory_space=pltpu.HBM)] * count,
        out_specs=[pl.BlockSpec(memory_space=pltpu.HBM)] * count,
        out_shape=[jax.ShapeDtypeStruct(a.shape, t) for a, t in zip(arrays, types_out)],
        scratch_shapes=[pltpu.VMEM(a.shape, a.dtype) for a in arrays]
        + [
            pltpu.VMEM(arrays[-1].shape, F32),
            pltpu.SemaphoreType.DMA((count,)),
            pltpu.SemaphoreType.DMA((count,)),
        ],
        compiler_params=pltpu.CompilerParams(vmem_limit_bytes=VMEM_LIMIT),
    )(*arrays)


def local(
    query_short,
    key_short,
    value_short,
    short_taps,
    query_long,
    key_long,
    long_residue,
    long_rate,
    cotangent,
):
    count = lax.axis_size("ctx")
    tokens_here, channels = query_short.shape
    modes = long_rate.shape[0]
    sequence = tokens_here * count
    planes = count // 4
    rows = count // ROW
    own_lanes = channels // ROW

    forward = forward_table()
    inputs = {
        "long_rate": long_rate,
        "query_long": query_long,
        "cotangent": cotangent,
        "key_short": key_short,
        "value_short": value_short,
        "long_residue": long_residue,
        "forward_three": jnp.asarray(three_terms(forward[:, :T])),
        "inverse_low": jnp.asarray(three_terms(inverse_table(np.arange(T)))),
        "short_taps": short_taps,
        "key_long": key_long,
        "query_short": query_short,
        "forward_two": jnp.asarray(two_terms(forward[:, :T])),
        "forward_full": jnp.asarray(two_terms(forward)),
        "inverse_high": jnp.asarray(three_terms(inverse_table(np.arange(T) + T))),
        "inverse_lags": jnp.asarray(three_terms(inverse_table(T - np.arange(T)))),
    }
    tokens = (tokens_here, channels)
    outputs = {
        "core_output": (tokens, BF16),
        "query_short_grad": (tokens, BF16),
        "key_short_grad": (tokens, BF16),
        "value_short_grad": (tokens, BF16),
        "query_long_grad": (tokens, BF16),
        "key_long_grad": (tokens, BF16),
        "taps_grad": (short_taps.shape, BF16),
    }
    scratch = {name: pltpu.VMEM(array.shape, array.dtype) for name, array in inputs.items()}
    for name, (shape, dtype) in outputs.items():
        scratch[name] = pltpu.VMEM(shape, dtype)
    for name in ("steps", "rise", "fall"):
        scratch[name] = pltpu.VMEM((modes, 8, channels), F32)
    scratch["store_sems"] = pltpu.SemaphoreType.DMA((len(outputs),))
    scratch["load_sems"] = pltpu.SemaphoreType.DMA((len(inputs),))
    state = (modes, own_lanes)
    for name in ("later", "earlier"):
        for part in ("sums", "row", "local", "out", "got"):
            scratch[name + "_" + part] = pltpu.VMEM((ROW,) + state, F32)
        scratch[name + "_total"] = pltpu.VMEM(state, F32)
        scratch[name + "_rows"] = pltpu.VMEM((rows,) + state, F32)
        scratch[name + "_sems"] = pltpu.SemaphoreType.DMA((4,))
        scratch[name + "_row_sems"] = pltpu.SemaphoreType.DMA((2, rows))
    scratch["extended"] = pltpu.VMEM((2 * T, channels), BF16)
    scratch["back_ext"] = pltpu.VMEM((2 * T, channels), BF16)
    scratch["long_grad"] = pltpu.VMEM(tokens, BF16)
    scratch["long_input"] = pltpu.VMEM(tokens, BF16)
    scratch["long_part"] = pltpu.VMEM(tokens, F32)
    scratch["block_scr"] = pltpu.VMEM((T, WIDTH), F32)
    for name in ("filter_spec", "taps_spec", "input_spec", "own_spec"):
        scratch[name] = pltpu.VMEM((N, channels), F32)
    scratch["lags"] = pltpu.VMEM((T, channels), F32)
    scratch["half_scr"] = pltpu.VMEM((T, channels // 2), F32)
    tile = (2 * T // planes, channels // 4)
    scratch["sum_scr"] = pltpu.VMEM((planes,) + tile, BF16)
    scratch["plane_scr"] = pltpu.VMEM((planes,) + tile, BF16)
    scratch["own_scr"] = pltpu.VMEM(tile, F32)
    scratch["pair_scr"] = pltpu.VMEM(tile, F32)
    for name in ("front", "behind"):
        for part in ("_held", "_passed"):
            scratch[name + part] = pltpu.VMEM((T, channels // ROW), BF16)
        scratch[name + "_sems"] = pltpu.SemaphoreType.DMA((7,))
    scratch["lag_sems"] = pltpu.SemaphoreType.DMA((2, 5))

    names = [name + "_hbm" for name in inputs] + [name + "_out" for name in outputs]
    names += list(scratch)
    results = pl.pallas_call(
        functools.partial(
            core_kernel,
            names=tuple(names),
            loads=tuple(inputs),
            count=count,
            scale=sequence**-0.5,
        ),
        in_specs=[pl.BlockSpec(memory_space=pltpu.HBM)] * len(inputs),
        out_specs=[pl.BlockSpec(memory_space=pltpu.HBM)] * len(outputs),
        out_shape=[jax.ShapeDtypeStruct(shape, dtype) for shape, dtype in outputs.values()],
        scratch_shapes=list(scratch.values()),
        compiler_params=pltpu.CompilerParams(
            collective_id=0, has_side_effects=True, vmem_limit_bytes=VMEM_LIMIT
        ),
    )(*inputs.values())
    return tuple(stored(results))


def solution(mesh):
    tokens = P("ctx", "ch")
    table = P(None, "ch")
    return jax.shard_map(
        local,
        mesh=mesh,
        in_specs=(tokens, tokens, tokens, table, tokens, tokens, table, table, tokens),
        out_specs=(tokens, tokens, tokens, tokens, tokens, tokens, table),
        check_vma=False,
    )
```
